32 devices in a mesh: dp: 4 (over y, core), seq: 8 (over z, x).
Axes of the slice: x: 2, y: 2, z: 4, core: 2. Of those that a mesh axis runs over, the one named last changes fastest.
Arguments:
- layer_input: bfloat16 [4096, 8192], P(('dp', 'seq')), may hold values from -6 to 6
- queries: bfloat16 [4096, 4096], P(('dp', 'seq')), may hold values from -110 to 110, as said below
- key_states: bfloat16 [4096, 512], P(('dp', 'seq')), may hold values from -12 to 12, as said below
- value_states: bfloat16 [4096, 512], P(('dp', 'seq')), may hold values from -6 to 6
- out_grad: bfloat16 [4096, 4096], P(('dp', 'seq')), may hold values from -6 to 6
Outputs:
- query_grad: bfloat16 [4096, 4096], P(('dp', 'seq'))
- key_grad: bfloat16 [4096, 512], P(('dp', 'seq'))
- value_grad: bfloat16 [4096, 512], P(('dp', 'seq'))
- weight_grad: float32 [8192, 1024], P(('dp', 'seq'))
The draws below stay inside these ranges and needn't reach their ends.
Inputs may be any that keep to these rules, and one draw needn't show every extreme that they name: `queries`: rows of rough scales; some queries may nearly coincide in direction with keys of earlier positions. `key_states`: rows of rough scales.
All inputs are finite; a program needn't handle non-finite values.
Results may differ from the reference program's by a relative error of at most 0.0051.
Values may be sent and summed in bfloat16 or wider, within the bound.
No kernel may reach another device: no remote copies, remote signals or barrier semaphores. Data moves between devices by JAX's collectives and lax.ppermute only.
A program may use at most 128 MiB of HBM per device.

```python
import math
import jax
import jax.numpy as jnp
from jax import lax

D = 8192
QH = 32
KVH = 4
HD = 128
SEQ_LEN = 1024
TOKENS = 4096
N_DP = 4


def rough_rows(key, shape, lowest, highest):
    scales = jnp.exp(jax.random.uniform(jax.random.fold_in(key, 21), (shape[0], 1), minval=math.log(lowest), maxval=math.log(highest)))
    entries = jax.random.truncated_normal(jax.random.fold_in(key, 22), -4.0, 4.0, shape)
    return (entries * scales).astype(jnp.float32)


def draw_queries(key, part):
    result = rough_rows(jax.random.fold_in(key, 4), (TOKENS, QH * HD), 0.5, 2.0)
    return result.astype(jnp.bfloat16)


def draw_key_states(key, part):
    result = rough_rows(jax.random.fold_in(key, 5), (TOKENS, KVH * HD), 0.3, 3.0)
    return result.astype(jnp.bfloat16)


def spiked(values, stream_key, source, target, blocks, factor):
    owner, partner = [(jnp.arange(values.shape[position]) // (values.shape[position] // blocks)).reshape([-1 if axis == position else 1 for axis in range(values.ndim)]) for position in (source, target)]
    chosen = jax.random.permutation(stream_key, blocks)[partner]
    strong = (owner == chosen) | (owner == (partner + blocks // 2) % blocks)
    return jnp.where(strong, factor * values, values)


def level_of(own_key, shape, split, least, top_value):
    level = 1.0
    for axis_at, parts in split:
        draws = jax.random.uniform(jax.random.fold_in(jax.random.fold_in(own_key, 6), axis_at), (parts,), jnp.float32, least / len(split), top_value / len(split))
        level = level * jnp.repeat(jnp.exp(draws), shape[axis_at] // parts).reshape((-1,) + (1,) * (len(shape) - 1 - axis_at))
    return level


def gaussian(rng, extent, spread, most, pieces=(), kind=jnp.bfloat16):
    array = spread * jax.random.normal(rng, extent, jnp.float32)
    if pieces:
        array = array * level_of(rng, extent, pieces, -0.22, 0.18)
    return jnp.clip(array, -most, most).astype(kind)


def bell_draw_with(stream_key, extent, width, most, pieces, heavy, kind=jnp.bfloat16):
    values = width * jax.random.normal(stream_key, extent, jnp.float32)
    if pieces:
        values = values * level_of(stream_key, extent, pieces, -0.22, 0.18)
    return jnp.clip(spiked(values, jax.random.fold_in(stream_key, 3), *heavy), -most, most).astype(kind)


def setup_inputs(seed: int = 0) -> dict:
    splits = jax.random.split(jax.random.key(seed), 6)
    layer_input = bell_draw_with(splits[0], (TOKENS, D), 1.0, 6.0, ((0, 32),), (0, 1, 32, 2.75))
    queries = draw_queries(jax.random.fold_in(splits[5], 71), 0)
    key_states = draw_key_states(jax.random.fold_in(splits[5], 71), 0)
    value_states = gaussian(splits[3], (TOKENS, KVH * HD), 1.0, 6.0, ((0, 32),))
    out_grad = gaussian(splits[4], (TOKENS, QH * HD), 1.0, 6.0, ((0, 32),))
    return dict(layer_input=layer_input, queries=queries, key_states=key_states, value_states=value_states, out_grad=out_grad)


NEGATIVE = -1e+30

def head_grads(operands):
    query_block, key_block, value_block, grad_block = operands
    scale = 1.0 / math.sqrt(HD)
    places = jnp.arange(SEQ_LEN, dtype=jnp.int32)
    visible = places[None, :] <= places[:, None]
    scores = jnp.einsum('gtd,sd->gts', query_block, key_block) * scale
    scores = jnp.where(visible[None], scores, NEGATIVE)
    row_max = lax.optimization_barrier(jnp.max(scores, axis=-1, keepdims=True))
    expon = jnp.exp(scores - row_max)
    denom = lax.optimization_barrier(jnp.sum(expon, axis=-1, keepdims=True))
    grad_probs = jnp.einsum('gtd,sd->gts', grad_block, value_block)
    delta = lax.optimization_barrier(jnp.sum(expon * grad_probs, axis=-1, keepdims=True)) / denom
    probs = jnp.exp(scores - row_max) / denom
    grad_scores = lax.optimization_barrier((scale * probs * (grad_probs - delta)).astype(jnp.bfloat16))
    probs_low = lax.optimization_barrier(probs.astype(jnp.bfloat16))
    grad_scores = grad_scores.astype(jnp.float32)
    probs_low = probs_low.astype(jnp.float32)
    query_part = jnp.einsum('gts,sd->gtd', grad_scores, key_block)
    key_part = jnp.einsum('gts,gtd->sd', grad_scores, query_block)
    value_part = jnp.einsum('gts,gtd->sd', probs_low, grad_block)
    return (query_part, key_part, value_part)

def sequence_grads(operands):
    queries, key_states, value_states, out_grad = operands
    group = QH // KVH
    query_heads = jnp.transpose(queries.astype(jnp.float32).reshape(SEQ_LEN, KVH, group, HD), (1, 2, 0, 3))
    grad_heads = jnp.transpose(out_grad.astype(jnp.float32).reshape(SEQ_LEN, KVH, group, HD), (1, 2, 0, 3))
    key_heads = jnp.transpose(key_states.astype(jnp.float32).reshape(SEQ_LEN, KVH, HD), (1, 0, 2))
    value_heads = jnp.transpose(value_states.astype(jnp.float32).reshape(SEQ_LEN, KVH, HD), (1, 0, 2))
    query_part, key_part, value_part = lax.map(head_grads, (query_heads, key_heads, value_heads, grad_heads))
    query_grad = jnp.transpose(query_part, (2, 0, 1, 3)).reshape(SEQ_LEN, QH * HD).astype(jnp.bfloat16)
    key_grad = jnp.transpose(key_part, (1, 0, 2)).reshape(SEQ_LEN, KVH * HD).astype(jnp.bfloat16)
    value_grad = jnp.transpose(value_part, (1, 0, 2)).reshape(SEQ_LEN, KVH * HD).astype(jnp.bfloat16)
    return (query_grad, key_grad, value_grad)

def reference(layer_input, queries, key_states, value_states, out_grad):
    query_grad, key_grad, value_grad = lax.map(sequence_grads, (queries.reshape(N_DP, SEQ_LEN, QH * HD), key_states.reshape(N_DP, SEQ_LEN, KVH * HD), value_states.reshape(N_DP, SEQ_LEN, KVH * HD), out_grad.reshape(N_DP, SEQ_LEN, QH * HD)))
    query_grad = query_grad.reshape(TOKENS, QH * HD)
    key_grad = key_grad.reshape(TOKENS, KVH * HD)
    value_grad = value_grad.reshape(TOKENS, KVH * HD)
    both_grads = jnp.concatenate([key_grad, value_grad], axis=1)
    weight_grad = jnp.dot(layer_input.T, both_grads, preferred_element_type=jnp.float32)
    return (query_grad, key_grad, value_grad, weight_grad)
```

```python
import math

import jax
import jax.numpy as jnp
from jax import lax
from jax.experimental import pallas as pl
from jax.experimental.pallas import tpu as pltpu
from jax.sharding import PartitionSpec as P

D = 8192
QH = 32
KVH = 4
HD = 128
GROUP = QH // KVH
WIDE = GROUP * HD
TILE = 256
NEGATIVE = -1e30
BF16 = jnp.bfloat16
F32 = jnp.float32
VMEM_BYTES = 48 * 1024 * 1024

NT = (((1,), (1,)), ((), ()))


def attention_kernel(rows, groups, *refs):
    span = KVH * rows
    q_hbm, do_hbm, k_hbm, v_hbm = refs[:4]
    pieces = refs[4 : 4 + KVH - 1]
    at = 4 + KVH - 1
    earlier = refs[at : at + KVH * (groups - 1)]
    at += KVH * (groups - 1)
    dq_out = refs[at : at + KVH]
    at += KVH
    own_out = refs[at]
    at += 1
    down_out = refs[at : at + groups - 1]
    at += groups - 1
    q_s, do_s, k_s, v_s, kt_s, dq_s, dk_s, dv_s, down_s, sems = refs[at:]

    place = lax.axis_index("seq")
    group = place // KVH
    head = place % KVH

    def row_at(k, base=0):
        return pl.ds(pl.multiple_of(base + (head ^ k) * rows, rows), rows)

    def column_at(block):
        return pl.ds(pl.multiple_of(head * block, block), block)

    copies = [
        pltpu.make_async_copy(q_hbm.at[:, column_at(WIDE)], q_s.at[row_at(0)], sems.at[0]),
        pltpu.make_async_copy(do_hbm.at[:, column_at(WIDE)], do_s.at[row_at(0)], sems.at[1]),
        pltpu.make_async_copy(k_hbm.at[:, column_at(HD)], k_s.at[row_at(0, group * span)], sems.at[2]),
        pltpu.make_async_copy(v_hbm.at[:, column_at(HD)], v_s.at[row_at(0, group * span)], sems.at[3]),
    ]
    for k in range(1, KVH):
        piece = pieces[k - 1]
        slot = 4 * k
        copies += [
            pltpu.make_async_copy(piece.at[:, :WIDE], q_s.at[row_at(k)], sems.at[slot]),
            pltpu.make_async_copy(piece.at[:, WIDE : 2 * WIDE], do_s.at[row_at(k)], sems.at[slot + 1]),
            pltpu.make_async_copy(
                piece.at[:, 2 * WIDE : 2 * WIDE + HD], k_s.at[row_at(k, group * span)], sems.at[slot + 2]
            ),
            pltpu.make_async_copy(
                piece.at[:, 2 * WIDE + HD :], v_s.at[row_at(k, group * span)], sems.at[slot + 3]
            ),
        ]
    for copy in copies:
        copy.start()
    slot = 4 * KVH
    for step in range(1, groups):
        source = (group + groups - step) % groups
        for k in range(KVH):
            piece = earlier[(step - 1) * KVH + k]

            @pl.when(group >= step)
            def _(piece=piece, k=k, slot=slot, source=source):
                first = pltpu.make_async_copy(
                    piece.at[:, :HD], k_s.at[row_at(k, source * span)], sems.at[slot]
                )
                second = pltpu.make_async_copy(
                    piece.at[:, HD:], v_s.at[row_at(k, source * span)], sems.at[slot + 1]
                )
                first.start()
                second.start()
                first.wait()
                second.wait()

            slot += 2
    for copy in copies:
        copy.wait()

    dk_s[...] = jnp.zeros_like(dk_s)
    dv_s[...] = jnp.zeros_like(dv_s)
    scale = 1.0 / math.sqrt(HD)
    fold = scale * math.log2(math.e)

    for which in range(groups):

        @pl.when(group == which)
        def _(which=which):
            for block in range((which + 1) * span // TILE):
                keys = slice(block * TILE, (block + 1) * TILE)
                kt_s[:, keys] = k_s[keys, :].T

            def one_head(h, carry):
                columns = pl.ds(pl.multiple_of(h * HD, HD), HD)
                for part in range(span // TILE):
                    q = q_s[part * TILE : (part + 1) * TILE, columns]
                    do = do_s[part * TILE : (part + 1) * TILE, columns]
                    length = which * span + (part + 1) * TILE
                    blocks = length // TILE
                    scores = []
                    grads = []
                    for b in range(blocks):
                        keys = slice(b * TILE, (b + 1) * TILE)
                        one = lax.dot_general(k_s[keys, :], q, NT, preferred_element_type=F32)
                        if b == blocks - 1:
                            key_place = lax.broadcasted_iota(jnp.int32, (TILE, TILE), 0)
                            query_place = lax.broadcasted_iota(jnp.int32, (TILE, TILE), 1)
                            one = jnp.where(key_place <= query_place, one, NEGATIVE)
                        scores.append(one)
                        grads.append(
                            lax.dot_general(v_s[keys, :], do, NT, preferred_element_type=F32)
                        )
                    top = scores[0].max(axis=0, keepdims=True)
                    for one in scores[1:]:
                        top = jnp.maximum(top, one.max(axis=0, keepdims=True))
                    expon = [jnp.exp2((one - top) * fold) for one in scores]
                    denom = sum(e.sum(axis=0, keepdims=True) for e in expon)
                    weighted = sum(
                        (e * gp).sum(axis=0, keepdims=True) for e, gp in zip(expon, grads)
                    )
                    inverse = 1.0 / denom
                    delta = weighted * inverse
                    probs = jnp.concatenate([(e * inverse).astype(BF16) for e in expon], axis=0)
                    grad_scores = jnp.concatenate(
                        [
                            (e * (inverse * scale) * (gp - delta)).astype(BF16)
                            for e, gp in zip(expon, grads)
                        ],
                        axis=0,
                    )
                    dv_s[:length, :] += jnp.dot(probs, do, preferred_element_type=F32)
                    dk_s[:length, :] += jnp.dot(grad_scores, q, preferred_element_type=F32)
                    dqt = jnp.dot(kt_s[:, :length], grad_scores, preferred_element_type=F32)
                    dq_s[part * TILE : (part + 1) * TILE, columns] = dqt.T.astype(BF16)
                return carry

            lax.fori_loop(0, GROUP, one_head, 0)
            base = which * span
            own_out[:, :HD] = dk_s[base : base + span, :]
            own_out[:, HD:] = dv_s[base : base + span, :]
            for step in range(1, which + 1):
                source = (which - step) * span
                down_s[step - 1, :, :HD] = dk_s[source : source + span, :].astype(BF16)
                down_s[step - 1, :, HD:] = dv_s[source : source + span, :].astype(BF16)
            for step in range(which + 1, groups):
                down_s[step - 1] = jnp.zeros((span, 2 * HD), BF16)

    outs = [pltpu.make_async_copy(dq_s.at[row_at(k)], dq_out[k], sems.at[k]) for k in range(KVH)]
    outs += [
        pltpu.make_async_copy(down_s.at[step], down_out[step], sems.at[KVH + step])
        for step in range(groups - 1)
    ]
    for copy in outs:
        copy.start()
    for copy in outs:
        copy.wait()


def attention(rows, groups, queries, out_grad, key_states, value_states, pieces, earlier):
    span = KVH * rows
    length = groups * span
    any_spec = pl.BlockSpec(memory_space=pl.ANY)
    n_in = 4 + len(pieces) + len(earlier)
    out_shape = (
        [jax.ShapeDtypeStruct((rows, WIDE), BF16)] * KVH
        + [jax.ShapeDtypeStruct((span, 2 * HD), F32)]
        + [jax.ShapeDtypeStruct((span, 2 * HD), BF16)] * (groups - 1)
    )
    out_specs = (
        [any_spec] * KVH
        + [pl.BlockSpec(memory_space=pltpu.VMEM)]
        + [any_spec] * (groups - 1)
    )
    outs = pl.pallas_call(
        lambda *refs: attention_kernel(rows, groups, *refs),
        out_shape=out_shape,
        in_specs=[any_spec] * n_in,
        out_specs=out_specs,
        scratch_shapes=[
            pltpu.VMEM((span, WIDE), BF16),
            pltpu.VMEM((span, WIDE), BF16),
            pltpu.VMEM((length, HD), BF16),
            pltpu.VMEM((length, HD), BF16),
            pltpu.VMEM((HD, length), BF16),
            pltpu.VMEM((span, WIDE), BF16),
            pltpu.VMEM((length, HD), F32),
            pltpu.VMEM((length, HD), F32),
            pltpu.VMEM((max(groups - 1, 1), span, 2 * HD), BF16),
            pltpu.SemaphoreType.DMA((4 * KVH + 2 * KVH * groups,)),
        ],
        compiler_params=pltpu.CompilerParams(vmem_limit_bytes=VMEM_BYTES),
        cost_estimate=pl.CostEstimate(flops=10**10, bytes_accessed=5 * 10**7, transcendentals=0),
        name="attention",
    )(queries, out_grad, key_states, value_states, *pieces, *earlier)
    return outs[:KVH], outs[KVH], outs[KVH + 1 :]


def transpose_kernel(rows, blocks, slab, *refs):
    pieces = refs[:KVH]
    out = refs[KVH]
    x_s, sems = refs[KVH + 1 :]
    head = lax.axis_index("seq") % KVH
    span = KVH * rows
    copies = []
    for k in range(KVH):
        for core in range(2):
            copies.append(
                pltpu.make_async_copy(
                    pieces[k].at[core * rows : (core + 1) * rows],
                    x_s.at[pl.ds(pl.multiple_of(core * span + (head ^ k) * rows, rows), rows)],
                    sems.at[2 * k + core],
                )
            )
    for copy in copies:
        copy.start()
    for copy in copies:
        copy.wait()
    width = x_s.shape[1]
    for a in range(width // TILE):
        for b in range(2 * span // TILE):
            out[a * TILE : (a + 1) * TILE, b * TILE : (b + 1) * TILE] = x_s[
                b * TILE : (b + 1) * TILE, a * TILE : (a + 1) * TILE
            ].T


def transposed(rows, blocks, slab, pieces):
    width = pieces[0].shape[1]
    tokens = 2 * KVH * rows
    return pl.pallas_call(
        lambda *refs: transpose_kernel(rows, blocks, slab, *refs),
        out_shape=jax.ShapeDtypeStruct((width, tokens), BF16),
        in_specs=[pl.BlockSpec(memory_space=pl.ANY)] * KVH,
        out_specs=pl.BlockSpec(memory_space=pltpu.VMEM),
        scratch_shapes=[pltpu.VMEM((tokens, width), BF16), pltpu.SemaphoreType.DMA((2 * KVH,))],
        compiler_params=pltpu.CompilerParams(vmem_limit_bytes=VMEM_BYTES),
        cost_estimate=pl.CostEstimate(flops=0, bytes_accessed=10**7, transcendentals=0),
        name="input_transposed",
    )(*pieces)


def weight_kernel(rows, halves, groups, slab, *refs):
    span = KVH * rows
    own = refs[:KVH]
    other = refs[KVH : 2 * KVH]
    xt = refs[2 * KVH]
    keep, send, key_out, value_out = refs[2 * KVH + 1 : 2 * KVH + 5]
    g_s, sems = refs[2 * KVH + 5 :]
    place = lax.axis_index("seq")
    group = place // KVH
    head = place % KVH
    half = lax.axis_index("dp") // 2
    channels = KVH * HD
    copies = []
    slot = 0
    for k in range(KVH):
        for core, piece in ((0, own[k]), (1, other[k])):
            for kind in range(2):
                copies.append(
                    pltpu.make_async_copy(
                        piece.at[:, kind * HD : (kind + 1) * HD],
                        g_s.at[
                            core * span : (core + 1) * span,
                            pl.ds(pl.multiple_of(kind * channels + (head ^ k) * HD, HD), HD),
                        ],
                        sems.at[slot],
                    )
                )
                slot += 1
    for copy in copies:
        copy.start()
    for copy in copies:
        copy.wait()
    mine = pl.ds(pl.multiple_of(head * rows, rows), rows)
    key_out[...] = g_s[mine, :channels]
    value_out[...] = g_s[mine, channels:]
    for apart in range(halves):
        for step in range(groups):
            owner = ((half ^ apart) * groups + (group ^ step)) * slab
            left = xt[pl.ds(pl.multiple_of(owner, slab), slab), :]
            product = jnp.dot(left, g_s[...], preferred_element_type=F32)
            if apart == 0:
                keep[step * slab : (step + 1) * slab, :] = product
            else:
                first = ((apart - 1) * groups + step) * slab
                send[first : first + slab, :] = product.astype(BF16)


def weight_terms(rows, halves, groups, slab, own, other, xt):
    span = KVH * rows
    channels = 2 * KVH * HD
    vmem = pl.BlockSpec(memory_space=pltpu.VMEM)
    return pl.pallas_call(
        lambda *refs: weight_kernel(rows, halves, groups, slab, *refs),
        out_shape=[
            jax.ShapeDtypeStruct((groups * slab, channels), F32),
            jax.ShapeDtypeStruct((max(halves - 1, 1) * groups * slab, channels), BF16),
            jax.ShapeDtypeStruct((rows, channels // 2), BF16),
            jax.ShapeDtypeStruct((rows, channels // 2), BF16),
        ],
        in_specs=[pl.BlockSpec(memory_space=pl.ANY)] * (2 * KVH) + [vmem],
        out_specs=[vmem] * 4,
        scratch_shapes=[pltpu.VMEM((2 * span, channels), BF16), pltpu.SemaphoreType.DMA((4 * KVH,))],
        compiler_params=pltpu.CompilerParams(vmem_limit_bytes=VMEM_BYTES),
        cost_estimate=pl.CostEstimate(flops=3 * 10**9, bytes_accessed=10**7, transcendentals=0),
        name="weight_terms",
    )(*own, *other, xt)


def place_kernel(*refs):
    pieces = refs[:KVH]
    out, sems = refs[KVH:]
    head = lax.axis_index("seq") % KVH
    copies = [
        pltpu.make_async_copy(
            pieces[k],
            out.at[:, pl.ds(pl.multiple_of((head ^ k) * WIDE, WIDE), WIDE)],
            sems.at[k],
        )
        for k in range(KVH)
    ]
    for copy in copies:
        copy.start()
    for copy in copies:
        copy.wait()


def placed(rows, pieces):
    any_spec = pl.BlockSpec(memory_space=pl.ANY)
    return pl.pallas_call(
        place_kernel,
        out_shape=jax.ShapeDtypeStruct((rows, QH * HD), BF16),
        in_specs=[any_spec] * KVH,
        out_specs=any_spec,
        scratch_shapes=[pltpu.SemaphoreType.DMA((KVH,))],
        cost_estimate=pl.CostEstimate(flops=0, bytes_accessed=10**7, transcendentals=0),
        name="query_grad_placed",
    )(*pieces)


def local(layer_input, queries, key_states, value_states, out_grad):
    rows = layer_input.shape[0]
    cycle = lax.axis_size("seq")
    replicas = lax.axis_size("dp")
    groups = cycle // KVH
    halves = replicas // 2
    slab = D // (replicas * cycle)
    place = lax.axis_index("seq")
    head = place % KVH
    core = lax.axis_index("dp") % 2

    def swap(array, k):
        return lax.ppermute(array, "seq", [(i, i ^ k) for i in range(cycle)])

    def across_cores(array):
        return lax.ppermute(array, "dp", [(i, i ^ 1) for i in range(replicas)])

    def columns(array, index, width):
        return lax.dynamic_slice_in_dim(array, index * width, width, 1)

    kv_of = [
        jnp.concatenate(
            [columns(key_states, head ^ k, HD), columns(value_states, head ^ k, HD)], axis=1
        )
        for k in range(KVH)
    ]
    earlier = []
    for step in range(1, groups):
        for k in range(KVH):
            pairs = [
                (i, ((i // KVH) + step) * KVH + ((i % KVH) ^ k))
                for i in range(cycle - step * KVH)
            ]
            earlier.append(lax.ppermute(kv_of[k], "seq", pairs))
    pieces = [
        swap(
            jnp.concatenate(
                [columns(queries, head ^ k, WIDE), columns(out_grad, head ^ k, WIDE), kv_of[k]],
                axis=1,
            ),
            k,
        )
        for k in range(1, KVH)
    ]

    width = cycle * slab

    def of_core(array, which):
        return jnp.concatenate(
            [columns(array, 2 * half + which, width) for half in range(halves)], axis=1
        )

    mine = of_core(layer_input, core)
    given = across_cores(of_core(layer_input, 1 - core))

    def of_head(array, index):
        return jnp.concatenate(
            [columns(array, block * KVH + index, slab) for block in range(halves * groups)], axis=1
        )

    both = [
        jnp.concatenate([of_head(mine, head ^ k), of_head(given, head ^ k)], axis=0)
        for k in range(KVH)
    ]
    both, pieces = lax.optimization_barrier((both, pieces))
    inputs = [both[0]] + [swap(both[k], k) for k in range(1, KVH)]

    grads, own, down = attention(
        rows, groups, queries, out_grad, key_states, value_states, pieces, earlier
    )
    for step in range(1, groups):
        pairs = [(i + step * KVH, i) for i in range(cycle - step * KVH)]
        own = own + lax.ppermute(down[step - 1], "seq", pairs).astype(F32)
    summed = own.astype(BF16)

    gathered = [summed] + [swap(summed, k) for k in range(1, KVH)]
    others = [across_cores(piece) for piece in gathered]
    xt = transposed(rows, halves * groups, slab, inputs)
    keep, send, key_grad, value_grad = weight_terms(
        rows, halves, groups, slab, gathered, others, xt
    )
    query_grad = placed(rows, [grads[0]] + [swap(grads[k], k) for k in range(1, KVH)])

    size = groups * slab
    for apart in range(1, halves):
        part = send[(apart - 1) * size : apart * size]
        keep = keep + lax.ppermute(
            part, "dp", [(i, i ^ (2 * apart)) for i in range(replicas)]
        ).astype(F32)
    weight_grad = keep[:slab]
    for step in range(1, groups):
        part = keep[step * slab : (step + 1) * slab].astype(BF16)
        weight_grad = weight_grad + swap(part, step * KVH).astype(F32)
    return (query_grad, key_grad, value_grad, weight_grad)


def solution(mesh):
    spec = P(("dp", "seq"), None)
    return jax.shard_map(
        local, mesh=mesh, in_specs=(spec,) * 5, out_specs=(spec,) * 4, check_vma=False
    )
```

```python
import math

import jax
import jax.numpy as jnp
from jax import lax
from jax.experimental import pallas as pl
from jax.experimental.pallas import tpu as pltpu
from jax.sharding import PartitionSpec as P

D = 8192
QH = 32
KVH = 4
HD = 128
GROUP = QH // KVH
WIDE = GROUP * HD
TILE = 256
NEGATIVE = -1e30
BF16 = jnp.bfloat16
F32 = jnp.float32
VMEM_BYTES = 48 * 1024 * 1024

NT = (((1,), (1,)), ((), ()))


def pack_kernel(rows, groups, slabs, slab, *refs):
    in_kernel = slab % HD == 0
    q_hbm, do_hbm, k_hbm, v_hbm = refs[:4]
    at = 4
    if in_kernel:
        x_hbm = refs[at]
        at += 1
    kv_out = refs[at]
    piece_out = refs[at + 1 : at + KVH]
    at += KVH
    if in_kernel:
        x_out = refs[at : at + KVH]
        at += KVH
        x_s = refs[at]
        at += 1
    kv_s, piece_s, sems, x_sems, out_sems = refs[at:]
    head = lax.axis_index("seq") % KVH

    def of(k, block, base=0):
        return pl.ds(pl.multiple_of(base + (head ^ k) * block, block), block)

    small = []
    large = []
    wide = []
    for k in range(KVH):
        small.append(
            [
                pltpu.make_async_copy(
                    array.at[:, k * HD : (k + 1) * HD],
                    kv_s.at[group * KVH + k, :, kind * HD : (kind + 1) * HD],
                    sems.at[(group * KVH + k) * 2 + kind],
                )
                for group in range(groups)
                for kind, array in enumerate((k_hbm, v_hbm))
            ]
        )
    base = 2 * KVH * groups
    for k in range(1, KVH):
        large.append(
            [
                pltpu.make_async_copy(
                    array.at[:, of(k, WIDE)],
                    piece_s.at[k - 1, :, kind * WIDE : (kind + 1) * WIDE],
                    sems.at[base + 2 * k + kind],
                )
                for kind, array in enumerate((q_hbm, do_hbm))
            ]
        )
    if in_kernel:
        for k in range(KVH):
            wide.append(
                [
                    pltpu.make_async_copy(
                        x_hbm.at[:, of(k, slab, block * KVH * slab)],
                        x_s.at[k, :, block * slab : (block + 1) * slab],
                        x_sems.at[k * slabs + block],
                    )
                    for block in range(slabs)
                ]
            )
    for copies in small + large + wide:
        for copy in copies:
            copy.start()
    outs = []

    def pass_on(copies, source, target):
        for copy in copies:
            copy.wait()
        outs.append(pltpu.make_async_copy(source, target, out_sems.at[len(outs)]))
        outs[-1].start()

    pass_on([copy for copies in small for copy in copies], kv_s, kv_out)
    for k in range(1, KVH):
        pass_on(large[k - 1], piece_s.at[k - 1], piece_out[k - 1])
    for k, copies in enumerate(wide):
        pass_on(copies, x_s.at[k], x_out[k])
    for copy in outs:
        copy.wait()


def packed(rows, groups, slabs, slab, queries, out_grad, key_states, value_states, layer_input):
    any_spec = pl.BlockSpec(memory_space=pl.ANY)
    cycle = KVH * groups
    in_kernel = slab % HD == 0
    wide = KVH if in_kernel else 0
    inputs = (queries, out_grad, key_states, value_states) + ((layer_input,) if in_kernel else ())
    outs = pl.pallas_call(
        lambda *refs: pack_kernel(rows, groups, slabs, slab, *refs),
        out_shape=[jax.ShapeDtypeStruct((cycle, rows, 2 * HD), BF16)]
        + [jax.ShapeDtypeStruct((rows, 2 * WIDE), BF16)] * (KVH - 1)
        + [jax.ShapeDtypeStruct((rows, slabs * slab), BF16)] * wide,
        in_specs=[any_spec] * len(inputs),
        out_specs=[any_spec] * (KVH + wide),
        scratch_shapes=([pltpu.VMEM((KVH, rows, slabs * slab), BF16)] if in_kernel else [])
        + [
            pltpu.VMEM((cycle, rows, 2 * HD), BF16),
            pltpu.VMEM((KVH - 1, rows, 2 * WIDE), BF16),
            pltpu.SemaphoreType.DMA((2 * cycle + 2 * KVH,)),
            pltpu.SemaphoreType.DMA((KVH * slabs,)),
            pltpu.SemaphoreType.DMA((2 * KVH,)),
        ],
        compiler_params=pltpu.CompilerParams(vmem_limit_bytes=VMEM_BYTES),
        cost_estimate=pl.CostEstimate(flops=0, bytes_accessed=8 * 10**6, transcendentals=0),
        name="first_sends",
    )(*inputs)
    if in_kernel:
        columns = outs[KVH:]
    else:
        head = lax.axis_index("seq") % KVH
        columns = [
            jnp.concatenate(
                [
                    lax.dynamic_slice_in_dim(
                        layer_input, (block * KVH + (head ^ k)) * slab, slab, 1
                    )
                    for block in range(slabs)
                ],
                axis=1,
            )
            for k in range(KVH)
        ]
    return outs[0], outs[1:KVH], columns


def attention_kernel(rows, groups, *refs):
    span = KVH * rows
    q_hbm, do_hbm, kv_hbm = refs[:3]
    pieces = refs[3 : 3 + KVH - 1]
    at = 3 + KVH - 1
    dq_out = refs[at]
    at += 1
    own_k, own_v = refs[at : at + 2]
    at += 2
    down_out = refs[at : at + 2 * (groups - 1)]
    at += 2 * (groups - 1)
    q_s, do_s, k_s, v_s, kt_s, dk_s, dv_s, down_s, sems = refs[at:]

    place = lax.axis_index("seq")
    group = place // KVH
    head = place % KVH

    def row_at(k, base=0):
        return pl.ds(pl.multiple_of(base + (head ^ k) * rows, rows), rows)

    def column_at(block):
        return pl.ds(pl.multiple_of(head * block, block), block)

    copies = [
        pltpu.make_async_copy(q_hbm.at[:, column_at(WIDE)], q_s.at[row_at(0)], sems.at[0]),
        pltpu.make_async_copy(do_hbm.at[:, column_at(WIDE)], do_s.at[row_at(0)], sems.at[1]),
    ]
    for kind, target in enumerate((k_s, v_s)):
        copies += [
            pltpu.make_async_copy(
                kv_hbm.at[source, :, kind * HD : (kind + 1) * HD],
                target.at[source * rows : (source + 1) * rows],
                sems.at[2 * KVH + 2 * source + kind],
            )
            for source in range(KVH * groups)
        ]
    for k in range(1, KVH):
        piece = pieces[k - 1]
        copies += [
            pltpu.make_async_copy(piece.at[:, :WIDE], q_s.at[row_at(k)], sems.at[2 * k]),
            pltpu.make_async_copy(piece.at[:, WIDE:], do_s.at[row_at(k)], sems.at[2 * k + 1]),
        ]
    for copy in copies:
        copy.start()
    for copy in copies:
        copy.wait()

    dk_s[...] = jnp.zeros_like(dk_s)
    dv_s[...] = jnp.zeros_like(dv_s)
    scale = 1.0 / math.sqrt(HD)
    fold = scale * math.log2(math.e)

    for which in range(groups):

        @pl.when(group == which)
        def _(which=which):
            for block in range((which + 1) * span // TILE):
                keys = slice(block * TILE, (block + 1) * TILE)
                kt_s[:, keys] = k_s[keys, :].T

            def one_head(h, carry):
                columns = pl.ds(pl.multiple_of(h * HD, HD), HD)
                for part in range(span // TILE):
                    q = q_s[part * TILE : (part + 1) * TILE, columns]
                    do = do_s[part * TILE : (part + 1) * TILE, columns]
                    length = which * span + (part + 1) * TILE
                    blocks = length // TILE
                    scores = []
                    grads = []
                    for b in range(blocks):
                        keys = slice(b * TILE, (b + 1) * TILE)
                        one = lax.dot_general(k_s[keys, :], q, NT, preferred_element_type=F32)
                        if b == blocks - 1:
                            key_place = lax.broadcasted_iota(jnp.int32, (TILE, TILE), 0)
                            query_place = lax.broadcasted_iota(jnp.int32, (TILE, TILE), 1)
                            one = jnp.where(key_place <= query_place, one, NEGATIVE)
                        scores.append(one)
                        grads.append(
                            lax.dot_general(v_s[keys, :], do, NT, preferred_element_type=F32)
                        )
                    top = scores[0].max(axis=0, keepdims=True)
                    for one in scores[1:]:
                        top = jnp.maximum(top, one.max(axis=0, keepdims=True))
                    expon = [jnp.exp2((one - top) * fold) for one in scores]
                    denom = sum(e.sum(axis=0, keepdims=True) for e in expon)
                    weighted = sum(
                        (e * gp).sum(axis=0, keepdims=True) for e, gp in zip(expon, grads)
                    )
                    inverse = 1.0 / denom
                    delta = weighted * inverse
                    probs = jnp.concatenate([(e * inverse).astype(BF16) for e in expon], axis=0)
                    grad_scores = jnp.concatenate(
                        [
                            (e * (inverse * scale) * (gp - delta)).astype(BF16)
                            for e, gp in zip(expon, grads)
                        ],
                        axis=0,
                    )
                    dv_s[:length, :] += jnp.dot(probs, do, preferred_element_type=F32)
                    dk_s[:length, :] += jnp.dot(grad_scores, q, preferred_element_type=F32)
                    dqt = jnp.dot(kt_s[:, :length], grad_scores, preferred_element_type=F32)
                    dq_out[part * TILE : (part + 1) * TILE, columns] = dqt.T.astype(BF16)
                return carry

            lax.fori_loop(0, GROUP, one_head, 0)
            base = which * span
            own_k[...] = dk_s[base : base + span, :]
            own_v[...] = dv_s[base : base + span, :]
            for step in range(1, which + 1):
                source = (which - step) * span
                down_s[2 * step - 2] = dk_s[source : source + span, :].astype(BF16)
                down_s[2 * step - 1] = dv_s[source : source + span, :].astype(BF16)
            for step in range(which + 1, groups):
                down_s[2 * step - 2] = jnp.zeros((span, HD), BF16)
                down_s[2 * step - 1] = jnp.zeros((span, HD), BF16)

    outs = [
        pltpu.make_async_copy(down_s.at[step], down_out[step], sems.at[step])
        for step in range(2 * (groups - 1))
    ]
    for copy in outs:
        copy.start()
    for copy in outs:
        copy.wait()


def attention(rows, groups, queries, out_grad, keys_values, pieces):
    span = KVH * rows
    length = groups * span
    any_spec = pl.BlockSpec(memory_space=pl.ANY)
    n_in = 3 + len(pieces)
    out_shape = (
        [jax.ShapeDtypeStruct((span, WIDE), BF16)]
        + [jax.ShapeDtypeStruct((span, HD), F32)] * 2
        + [jax.ShapeDtypeStruct((span, HD), BF16)] * (2 * (groups - 1))
    )
    out_specs = (
        [pl.BlockSpec(memory_space=pltpu.VMEM)] * 3
        + [any_spec] * (2 * (groups - 1))
    )
    outs = pl.pallas_call(
        lambda *refs: attention_kernel(rows, groups, *refs),
        out_shape=out_shape,
        in_specs=[any_spec] * n_in,
        out_specs=out_specs,
        scratch_shapes=[
            pltpu.VMEM((span, WIDE), BF16),
            pltpu.VMEM((span, WIDE), BF16),
            pltpu.VMEM((length, HD), BF16),
            pltpu.VMEM((length, HD), BF16),
            pltpu.VMEM((HD, length), BF16),
            pltpu.VMEM((length, HD), F32),
            pltpu.VMEM((length, HD), F32),
            pltpu.VMEM((2 * max(groups - 1, 1), span, HD), BF16),
            pltpu.SemaphoreType.DMA((2 * KVH + 2 * KVH * groups,)),
        ],
        compiler_params=pltpu.CompilerParams(vmem_limit_bytes=VMEM_BYTES),
        cost_estimate=pl.CostEstimate(flops=10**10, bytes_accessed=5 * 10**7, transcendentals=0),
        name="attention",
    )(queries, out_grad, keys_values, *pieces)
    down = outs[3:]
    return outs[0], outs[1:3], (down[0::2], down[1::2])


def transpose_kernel(rows, halves, width, *refs):
    pieces = refs[:KVH]
    outs = refs[KVH : KVH + 2]
    x_s, sems = refs[KVH + 2 :]
    head = lax.axis_index("seq") % KVH
    core = lax.axis_index("dp") % 2
    copies = [
        pltpu.make_async_copy(
            pieces[k],
            x_s.at[pl.ds(pl.multiple_of((head ^ k) * rows, rows), rows)],
            sems.at[k],
        )
        for k in range(KVH)
    ]
    for copy in copies:
        copy.start()
    for copy in copies:
        copy.wait()
    tile = min(TILE, width)
    for which, out in enumerate(outs):
        for half in range(halves):
            for a in range(width // tile):
                first = (2 * half + (core ^ which)) * width + a * tile
                columns = pl.ds(pl.multiple_of(first, tile), tile)
                out[half * width + a * tile : half * width + (a + 1) * tile, :] = x_s[:, columns].T


def transposed(rows, halves, width, pieces):
    tokens = KVH * rows
    vmem = pl.BlockSpec(memory_space=pltpu.VMEM)
    return pl.pallas_call(
        lambda *refs: transpose_kernel(rows, halves, width, *refs),
        out_shape=[jax.ShapeDtypeStruct((halves * width, tokens), BF16)] * 2,
        in_specs=[pl.BlockSpec(memory_space=pl.ANY)] * KVH,
        out_specs=[vmem] * 2,
        scratch_shapes=[
            pltpu.VMEM((tokens, 2 * halves * width), BF16),
            pltpu.SemaphoreType.DMA((KVH,)),
        ],
        compiler_params=pltpu.CompilerParams(vmem_limit_bytes=VMEM_BYTES),
        cost_estimate=pl.CostEstimate(flops=0, bytes_accessed=10**7, transcendentals=0),
        name="input_transposed",
    )(*pieces)


def weight_kernel(rows, halves, groups, slab, joins, *refs):
    own, other, xt, xt_other = refs[:4]
    at = 4
    if joins:
        before = refs[at]
        at += 1
    keep = refs[at]
    send = refs[at + 1 : at + 1 + groups]
    mine_out, g_s = refs[at + 1 + groups :]
    span = KVH * rows
    width = KVH * HD
    if joins:
        send[0][:, width:] = before[...]
    place = lax.axis_index("seq")
    group = place // KVH
    head = place % KVH
    half = lax.axis_index("dp") // 2
    for source in range(KVH):
        columns = slice(source * HD, (source + 1) * HD)
        g_s[:span, columns] = own[source]
        g_s[span:, columns] = other[source]
        mine_out[:, columns] = own[source, pl.ds(pl.multiple_of(head * rows, rows), rows), :]
    for apart in range(halves):
        for step in range(groups):
            owner = ((half ^ apart) * groups + (group ^ step)) * slab
            at = pl.ds(pl.multiple_of(owner, slab), slab)
            product = jnp.dot(xt[at, :], g_s[:span, :], preferred_element_type=F32) + jnp.dot(
                xt_other[at, :], g_s[span:, :], preferred_element_type=F32
            )
            if apart == 0:
                keep[step * slab : (step + 1) * slab, :] = product
            else:
                send[step][(apart - 1) * slab : apart * slab, :width] = product.astype(BF16)


def weight_terms(rows, halves, groups, slab, own, other, xt, xt_other, before=None):
    span = KVH * rows
    channels = KVH * HD
    vmem = pl.BlockSpec(memory_space=pltpu.VMEM)
    joins = before is not None
    more = [before] if joins else []
    outs = pl.pallas_call(
        lambda *refs: weight_kernel(rows, halves, groups, slab, joins, *refs),
        out_shape=[jax.ShapeDtypeStruct((groups * slab, channels), F32)]
        + [
            jax.ShapeDtypeStruct(
                (max(halves - 1, 1) * slab, channels * (1 + (joins and step == 0))), BF16
            )
            for step in range(groups)
        ]
        + [jax.ShapeDtypeStruct((rows, channels), BF16)],
        in_specs=[vmem] * (4 + joins),
        out_specs=[vmem] * (groups + 2),
        scratch_shapes=[pltpu.VMEM((2 * span, channels), BF16)],
        compiler_params=pltpu.CompilerParams(vmem_limit_bytes=VMEM_BYTES),
        cost_estimate=pl.CostEstimate(flops=15 * 10**8, bytes_accessed=6 * 10**6, transcendentals=0),
        name="weight_terms",
    )(own, other, xt, xt_other, *more)
    return outs[0], outs[1 : 1 + groups], outs[1 + groups]


def place_kernel(pieces, out):
    for head in range(KVH):
        out[:, head * WIDE : (head + 1) * WIDE] = pieces[head]


def placed(rows, pieces):
    vmem = pl.BlockSpec(memory_space=pltpu.VMEM)
    return pl.pallas_call(
        place_kernel,
        out_shape=jax.ShapeDtypeStruct((rows, QH * HD), BF16),
        in_specs=[vmem],
        out_specs=vmem,
        compiler_params=pltpu.CompilerParams(vmem_limit_bytes=VMEM_BYTES),
        cost_estimate=pl.CostEstimate(flops=0, bytes_accessed=5 * 10**6, transcendentals=0),
        name="query_grad_placed",
    )(pieces)


def join_kernel(wide, *refs):
    keep = refs[:2]
    both = refs[2 : 2 + wide]
    out = refs[-1]
    rest = refs[2 + wide : -1]
    count = len(rest) // 2
    slab, width = out.shape[0], out.shape[1] // 2
    for kind in range(2):
        at = slice(kind * width, (kind + 1) * width)
        total = keep[kind][:slab, :]
        for ref in both:
            total = total + ref[:, at].astype(F32)
        for ref in rest[kind * count : (kind + 1) * count]:
            total = total + ref[...].astype(F32)
        out[:, at] = total


def joined(slab, keep, both, rest):
    vmem = pl.BlockSpec(memory_space=pltpu.VMEM)
    return pl.pallas_call(
        lambda *refs: join_kernel(len(both), *refs),
        out_shape=jax.ShapeDtypeStruct((slab, 2 * keep[0].shape[1]), F32),
        in_specs=[vmem] * (2 + len(both) + len(rest)),
        out_specs=vmem,
        compiler_params=pltpu.CompilerParams(vmem_limit_bytes=VMEM_BYTES),
        cost_estimate=pl.CostEstimate(flops=0, bytes_accessed=3 * 10**6, transcendentals=0),
        name="weight_grad_joined",
    )(*keep, *both, *rest)


def local(layer_input, queries, key_states, value_states, out_grad):
    rows = layer_input.shape[0]
    cycle = lax.axis_size("seq")
    replicas = lax.axis_size("dp")
    groups = cycle // KVH
    halves = replicas // 2
    slab = D // (replicas * cycle)
    after = lax.optimization_barrier
    within = [[i + k for k in range(KVH)] for i in range(0, cycle, KVH)]

    def swap(array, k):
        return lax.ppermute(array, "seq", [(i, i ^ k) for i in range(cycle)])

    def across_cores(array):
        return lax.ppermute(array, "dp", [(i, i ^ 1) for i in range(replicas)])

    def exchange(array, parts=None):
        return lax.all_to_all(
            array, "seq", split_axis=0, concat_axis=0, tiled=True, axis_index_groups=parts
        )

    keys_values, sends, columns = packed(
        rows,
        groups,
        replicas * groups,
        slab,
        queries,
        out_grad,
        key_states,
        value_states,
        layer_input,
    )
    keys_values = exchange(keys_values)
    pieces = [swap(sends[k - 1], k) for k in range(1, KVH)]

    columns, pieces = after((columns, pieces))
    inputs = [columns[0]] + [swap(columns[k], k) for k in range(1, KVH - 1)]

    grads, own, down = attention(rows, groups, queries, out_grad, keys_values, pieces)
    last, inputs, down = after((columns[KVH - 1], inputs, down))
    inputs.append(swap(last, KVH - 1))

    gathered = [None, None]
    others = [None, None]
    for kind in (1, 0):
        total = own[kind]
        for step in range(1, groups):
            pairs = [(i + step * KVH, i) for i in range(cycle - step * KVH)]
            total = total + lax.ppermute(down[kind][step - 1], "seq", pairs).astype(F32)
        copies = jnp.broadcast_to(total.astype(BF16)[None], (KVH,) + total.shape)
        gathered[kind] = exchange(copies, within)
        others[kind] = across_cores(gathered[kind])
    xt, xt_give = transposed(rows, halves, groups * slab, inputs)
    xt_other = across_cores(xt_give)

    narrow = [None, None]
    keep = [None, None]
    send = [None, None]
    keep[1], send[1], narrow[1] = weight_terms(
        rows, halves, groups, slab, gathered[1], others[1], xt, xt_other
    )
    keep[0], send[0], narrow[0] = weight_terms(
        rows, halves, groups, slab, gathered[0], others[0], xt, xt_other, send[1][0]
    )

    def over_sequences(array):
        return [
            lax.ppermute(
                array[(apart - 1) * slab : apart * slab],
                "dp",
                [(i, i ^ (2 * apart)) for i in range(replicas)],
            )
            for apart in range(1, halves)
        ]

    received = []
    for kind in (0, 1):
        for step in range(1, groups):
            total = keep[kind][step * slab : (step + 1) * slab]
            for part in over_sequences(send[kind][step]):
                total = total + part.astype(F32)
            received.append(swap(total.astype(BF16), step * KVH))
    weight_grad = joined(slab, keep, over_sequences(send[0][0]), received)

    grads, _ = after((grads, gathered))
    returned = exchange(grads.reshape(KVH, rows, WIDE), within)
    query_grad = placed(rows, returned)
    return (query_grad, narrow[0], narrow[1], weight_grad)


def solution(mesh):
    spec = P(("dp", "seq"), None)
    return jax.shard_map(
        local, mesh=mesh, in_specs=(spec,) * 5, out_specs=(spec,) * 4, check_vma=False
    )
```

```python
import math

import jax
import jax.numpy as jnp
from jax import lax
from jax.experimental import pallas as pl
from jax.experimental.pallas import tpu as pltpu
from jax.sharding import PartitionSpec as P

D = 8192
QH = 32
KVH = 4
HD = 128
GROUP = QH // KVH
WIDE = GROUP * HD
TILE = 256
NEGATIVE = -1e30
BF16 = jnp.bfloat16
F32 = jnp.float32
VMEM_BYTES = 24 * 1024 * 1024
ALL_VMEM_BYTES = 62 * 1024 * 1024

NT = (((1,), (1,)), ((), ()))


def pack_kernel(rows, groups, slabs, slab, *refs):
    in_kernel = slab % HD == 0
    q_hbm, do_hbm, k_hbm, v_hbm = refs[:4]
    at = 4
    if in_kernel:
        x_hbm = refs[at]
        at += 1
    kv_out = refs[at]
    piece_out = refs[at + 1 : at + KVH]
    at += KVH
    if in_kernel:
        x_out = refs[at : at + KVH]
        at += KVH
        x_s = refs[at]
        at += 1
    kv_s, piece_s, sems, x_sems, out_sems = refs[at:]
    head = lax.axis_index("seq") % KVH

    def of(k, block, base=0):
        return pl.ds(pl.multiple_of(base + (head ^ k) * block, block), block)

    small = []
    large = []
    wide = []
    for k in range(KVH):
        small.append(
            [
                pltpu.make_async_copy(
                    array.at[:, k * HD : (k + 1) * HD],
                    kv_s.at[group * KVH + k, :, kind * HD : (kind + 1) * HD],
                    sems.at[(group * KVH + k) * 2 + kind],
                )
                for group in range(groups)
                for kind, array in enumerate((k_hbm, v_hbm))
            ]
        )
    base = 2 * KVH * groups
    for k in range(1, KVH):
        large.append(
            [
                pltpu.make_async_copy(
                    array.at[:, of(k, WIDE)],
                    piece_s.at[k - 1, :, kind * WIDE : (kind + 1) * WIDE],
                    sems.at[base + 2 * k + kind],
                )
                for kind, array in enumerate((q_hbm, do_hbm))
            ]
        )
    if in_kernel:
        for k in range(KVH):
            wide.append(
                [
                    pltpu.make_async_copy(
                        x_hbm.at[:, of(k, slab, block * KVH * slab)],
                        x_s.at[k, :, block * slab : (block + 1) * slab],
                        x_sems.at[k * slabs + block],
                    )
                    for block in range(slabs)
                ]
            )
    for copies in small + large + wide:
        for copy in copies:
            copy.start()
    outs = []

    def pass_on(copies, source, target):
        for copy in copies:
            copy.wait()
        outs.append(pltpu.make_async_copy(source, target, out_sems.at[len(outs)]))
        outs[-1].start()

    pass_on([copy for copies in small for copy in copies], kv_s, kv_out)
    for k in range(1, KVH):
        pass_on(large[k - 1], piece_s.at[k - 1], piece_out[k - 1])
    for k, copies in enumerate(wide):
        pass_on(copies, x_s.at[k], x_out[k])
    for copy in outs:
        copy.wait()


def packed(rows, groups, slabs, slab, queries, out_grad, key_states, value_states, layer_input):
    any_spec = pl.BlockSpec(memory_space=pltpu.HBM)
    cycle = KVH * groups
    in_kernel = slab % HD == 0
    wide = KVH if in_kernel else 0
    inputs = (queries, out_grad, key_states, value_states) + ((layer_input,) if in_kernel else ())
    outs = pl.pallas_call(
        lambda *refs: pack_kernel(rows, groups, slabs, slab, *refs),
        out_shape=[jax.ShapeDtypeStruct((cycle, rows, 2 * HD), BF16)]
        + [jax.ShapeDtypeStruct((rows, 2 * WIDE), BF16)] * (KVH - 1)
        + [jax.ShapeDtypeStruct((rows, slabs * slab), BF16)] * wide,
        in_specs=[any_spec] * len(inputs),
        out_specs=[any_spec] * (KVH + wide),
        scratch_shapes=([pltpu.VMEM((KVH, rows, slabs * slab), BF16)] if in_kernel else [])
        + [
            pltpu.VMEM((cycle, rows, 2 * HD), BF16),
            pltpu.VMEM((KVH - 1, rows, 2 * WIDE), BF16),
            pltpu.SemaphoreType.DMA((2 * cycle + 2 * KVH,)),
            pltpu.SemaphoreType.DMA((KVH * slabs,)),
            pltpu.SemaphoreType.DMA((2 * KVH,)),
        ],
        compiler_params=pltpu.CompilerParams(vmem_limit_bytes=ALL_VMEM_BYTES),
        cost_estimate=pl.CostEstimate(flops=0, bytes_accessed=8 * 10**6, transcendentals=0),
        name="first_sends",
    )(*inputs)
    if in_kernel:
        columns = outs[KVH:]
    else:
        head = lax.axis_index("seq") % KVH
        columns = [
            jnp.concatenate(
                [
                    lax.dynamic_slice_in_dim(
                        layer_input, (block * KVH + (head ^ k)) * slab, slab, 1
                    )
                    for block in range(slabs)
                ],
                axis=1,
            )
            for k in range(KVH)
        ]
    return outs[0], outs[1:KVH], columns


def attention_kernel(rows, groups, *refs):
    span = KVH * rows
    q_hbm, do_hbm, kv_hbm = refs[:3]
    pieces = refs[3 : 3 + KVH - 1]
    at = 3 + KVH - 1
    dq_out = refs[at]
    at += 1
    own_k, own_v = refs[at : at + 2]
    at += 2
    down_out = refs[at : at + groups - 1]
    at += groups - 1
    q_s, do_s, k_s, v_s, kt_s, dk_s, dv_s, down_s, sems = refs[at:]

    place = lax.axis_index("seq")
    group = place // KVH
    head = place % KVH

    def row_at(k, base=0):
        return pl.ds(pl.multiple_of(base + (head ^ k) * rows, rows), rows)

    def column_at(block):
        return pl.ds(pl.multiple_of(head * block, block), block)

    copies = [
        pltpu.make_async_copy(q_hbm.at[:, column_at(WIDE)], q_s.at[row_at(0)], sems.at[0]),
        pltpu.make_async_copy(do_hbm.at[:, column_at(WIDE)], do_s.at[row_at(0)], sems.at[1]),
    ]
    for kind, target in enumerate((k_s, v_s)):
        copies += [
            pltpu.make_async_copy(
                kv_hbm.at[source, :, kind * HD : (kind + 1) * HD],
                target.at[source * rows : (source + 1) * rows],
                sems.at[2 * KVH + 2 * source + kind],
            )
            for source in range(KVH * groups)
        ]
    for k in range(1, KVH):
        piece = pieces[k - 1]
        copies += [
            pltpu.make_async_copy(piece.at[:, :WIDE], q_s.at[row_at(k)], sems.at[2 * k]),
            pltpu.make_async_copy(piece.at[:, WIDE:], do_s.at[row_at(k)], sems.at[2 * k + 1]),
        ]
    for copy in copies:
        copy.start()
    for copy in copies:
        copy.wait()

    dk_s[...] = jnp.zeros_like(dk_s)
    dv_s[...] = jnp.zeros_like(dv_s)
    scale = 1.0 / math.sqrt(HD)
    fold = scale * math.log2(math.e)

    for which in range(groups):

        @pl.when(group == which)
        def _(which=which):
            for block in range((which + 1) * span // TILE):
                keys = slice(block * TILE, (block + 1) * TILE)
                kt_s[:, keys] = k_s[keys, :].T

            def one_head(h, carry):
                columns = pl.ds(pl.multiple_of(h * HD, HD), HD)
                for part in range(span // TILE):
                    q = q_s[part * TILE : (part + 1) * TILE, columns]
                    do = do_s[part * TILE : (part + 1) * TILE, columns]
                    length = which * span + (part + 1) * TILE
                    blocks = length // TILE
                    scores = []
                    grads = []
                    for b in range(blocks):
                        keys = slice(b * TILE, (b + 1) * TILE)
                        one = lax.dot_general(k_s[keys, :], q, NT, preferred_element_type=F32)
                        if b == blocks - 1:
                            key_place = lax.broadcasted_iota(jnp.int32, (TILE, TILE), 0)
                            query_place = lax.broadcasted_iota(jnp.int32, (TILE, TILE), 1)
                            one = jnp.where(key_place <= query_place, one, NEGATIVE)
                        scores.append(one)
                        grads.append(
                            lax.dot_general(v_s[keys, :], do, NT, preferred_element_type=F32)
                        )
                    top = scores[0].max(axis=0, keepdims=True)
                    for one in scores[1:]:
                        top = jnp.maximum(top, one.max(axis=0, keepdims=True))
                    expon = [jnp.exp2((one - top) * fold) for one in scores]
                    denom = sum(e.sum(axis=0, keepdims=True) for e in expon)
                    weighted = sum(
                        (e * gp).sum(axis=0, keepdims=True) for e, gp in zip(expon, grads)
                    )
                    inverse = 1.0 / denom
                    delta = weighted * inverse
                    probs = jnp.concatenate([(e * inverse).astype(BF16) for e in expon], axis=0)
                    grad_scores = jnp.concatenate(
                        [
                            (e * (inverse * scale) * (gp - delta)).astype(BF16)
                            for e, gp in zip(expon, grads)
                        ],
                        axis=0,
                    )
                    dv_s[:length, :] += jnp.dot(probs, do, preferred_element_type=F32)
                    dk_s[:length, :] += jnp.dot(grad_scores, q, preferred_element_type=F32)
                    dqt = jnp.dot(kt_s[:, :length], grad_scores, preferred_element_type=F32)
                    dq_out[part * TILE : (part + 1) * TILE, columns] = dqt.T.astype(BF16)
                return carry

            lax.fori_loop(0, GROUP, one_head, 0)
            base = which * span
            own_k[...] = dk_s[base : base + span, :]
            own_v[...] = dv_s[base : base + span, :]
            for step in range(1, which + 1):
                source = (which - step) * span
                down_s[step - 1, 0] = dk_s[source : source + span, :].astype(BF16)
                down_s[step - 1, 1] = dv_s[source : source + span, :].astype(BF16)
            for step in range(which + 1, groups):
                down_s[step - 1] = jnp.zeros((2, span, HD), BF16)

    outs = [
        pltpu.make_async_copy(down_s.at[step], down_out[step], sems.at[step])
        for step in range(groups - 1)
    ]
    for copy in outs:
        copy.start()
    for copy in outs:
        copy.wait()


def attention(rows, groups, queries, out_grad, keys_values, pieces):
    span = KVH * rows
    length = groups * span
    any_spec = pl.BlockSpec(memory_space=pltpu.HBM)
    n_in = 3 + len(pieces)
    out_shape = (
        [jax.ShapeDtypeStruct((span, WIDE), BF16)]
        + [jax.ShapeDtypeStruct((span, HD), F32)] * 2
        + [jax.ShapeDtypeStruct((2, span, HD), BF16)] * (groups - 1)
    )
    out_specs = (
        [pl.BlockSpec(memory_space=pltpu.VMEM)] * 3
        + [any_spec] * (groups - 1)
    )
    outs = pl.pallas_call(
        lambda *refs: attention_kernel(rows, groups, *refs),
        out_shape=out_shape,
        in_specs=[any_spec] * n_in,
        out_specs=out_specs,
        scratch_shapes=[
            pltpu.VMEM((span, WIDE), BF16),
            pltpu.VMEM((span, WIDE), BF16),
            pltpu.VMEM((length, HD), BF16),
            pltpu.VMEM((length, HD), BF16),
            pltpu.VMEM((HD, length), BF16),
            pltpu.VMEM((length, HD), F32),
            pltpu.VMEM((length, HD), F32),
            pltpu.VMEM((max(groups - 1, 1), 2, span, HD), BF16),
            pltpu.SemaphoreType.DMA((2 * KVH + 2 * KVH * groups,)),
        ],
        compiler_params=pltpu.CompilerParams(vmem_limit_bytes=ALL_VMEM_BYTES),
        cost_estimate=pl.CostEstimate(flops=10**10, bytes_accessed=5 * 10**7, transcendentals=0),
        name="attention",
    )(queries, out_grad, keys_values, *pieces)
    return outs[0], outs[1:3], outs[3:]


def transpose_kernel(rows, halves, width, *refs):
    pieces = refs[:KVH]
    outs = refs[KVH : KVH + 2]
    x_s, sems = refs[KVH + 2 :]
    head = lax.axis_index("seq") % KVH
    core = lax.axis_index("dp") % 2
    copies = [
        pltpu.make_async_copy(
            pieces[k],
            x_s.at[pl.ds(pl.multiple_of((head ^ k) * rows, rows), rows)],
            sems.at[k],
        )
        for k in range(KVH)
    ]
    for copy in copies:
        copy.start()
    for copy in copies:
        copy.wait()
    tile = min(TILE, width)
    for which, out in enumerate(outs):
        for half in range(halves):
            for a in range(width // tile):
                first = (2 * half + (core ^ which)) * width + a * tile
                columns = pl.ds(pl.multiple_of(first, tile), tile)
                out[half * width + a * tile : half * width + (a + 1) * tile, :] = x_s[:, columns].T


def transposed(rows, halves, width, pieces):
    tokens = KVH * rows
    vmem = pl.BlockSpec(memory_space=pltpu.VMEM)
    return pl.pallas_call(
        lambda *refs: transpose_kernel(rows, halves, width, *refs),
        out_shape=[jax.ShapeDtypeStruct((halves * width, tokens), BF16)] * 2,
        in_specs=[pl.BlockSpec(memory_space=pltpu.HBM)] * KVH,
        out_specs=[vmem] * 2,
        scratch_shapes=[
            pltpu.VMEM((tokens, 2 * halves * width), BF16),
            pltpu.SemaphoreType.DMA((KVH,)),
        ],
        compiler_params=pltpu.CompilerParams(vmem_limit_bytes=ALL_VMEM_BYTES),
        cost_estimate=pl.CostEstimate(flops=0, bytes_accessed=10**7, transcendentals=0),
        name="input_transposed",
    )(*pieces)


def weight_kernel(rows, halves, groups, slab, joins, *refs):
    own = refs[:KVH]
    other, xt, xt_other = refs[KVH : KVH + 3]
    at = KVH + 3
    if joins:
        before = refs[at]
        at += 1
    keep = refs[at]
    send = refs[at + 1 : at + 1 + groups]
    mine_out, g_s = refs[at + 1 + groups :]
    span = KVH * rows
    width = KVH * HD
    if joins:
        send[0][:, width:] = before[...]
    place = lax.axis_index("seq")
    group = place // KVH
    head = place % KVH
    half = lax.axis_index("dp") // 2
    for k in range(KVH):
        columns = pl.ds(pl.multiple_of((head ^ k) * HD, HD), HD)
        g_s[:span, columns] = own[k][...]
        g_s[span:, columns] = other[:, k * HD : (k + 1) * HD]
        mine_out[:, columns] = own[k][pl.ds(pl.multiple_of(head * rows, rows), rows), :]
    for apart in range(halves):
        for step in range(groups):
            owner = ((half ^ apart) * groups + (group ^ step)) * slab
            at = pl.ds(pl.multiple_of(owner, slab), slab)
            product = jnp.dot(xt[at, :], g_s[:span, :], preferred_element_type=F32) + jnp.dot(
                xt_other[at, :], g_s[span:, :], preferred_element_type=F32
            )
            if apart == 0:
                keep[step * slab : (step + 1) * slab, :] = product
            else:
                send[step][(apart - 1) * slab : apart * slab, :width] = product.astype(BF16)


def weight_terms(rows, halves, groups, slab, own, other, xt, xt_other, before=None):
    span = KVH * rows
    channels = KVH * HD
    vmem = pl.BlockSpec(memory_space=pltpu.VMEM)
    joins = before is not None
    more = [before] if joins else []
    outs = pl.pallas_call(
        lambda *refs: weight_kernel(rows, halves, groups, slab, joins, *refs),
        out_shape=[jax.ShapeDtypeStruct((groups * slab, channels), F32)]
        + [
            jax.ShapeDtypeStruct(
                (max(halves - 1, 1) * slab, channels * (1 + (joins and step == 0))), BF16
            )
            for step in range(groups)
        ]
        + [jax.ShapeDtypeStruct((rows, channels), BF16)],
        in_specs=[vmem] * (KVH + 3 + joins),
        out_specs=[vmem] * (groups + 2),
        scratch_shapes=[pltpu.VMEM((2 * span, channels), BF16)],
        compiler_params=pltpu.CompilerParams(vmem_limit_bytes=ALL_VMEM_BYTES),
        cost_estimate=pl.CostEstimate(flops=15 * 10**8, bytes_accessed=6 * 10**6, transcendentals=0),
        name="weight_terms",
    )(*own, other, xt, xt_other, *more)
    return outs[0], outs[1 : 1 + groups], outs[1 + groups]


def place_kernel(pieces, out):
    for head in range(KVH):
        out[:, head * WIDE : (head + 1) * WIDE] = pieces[head]


def placed(rows, pieces):
    vmem = pl.BlockSpec(memory_space=pltpu.VMEM)
    return pl.pallas_call(
        place_kernel,
        out_shape=jax.ShapeDtypeStruct((rows, QH * HD), BF16),
        in_specs=[vmem],
        out_specs=vmem,
        compiler_params=pltpu.CompilerParams(vmem_limit_bytes=ALL_VMEM_BYTES),
        cost_estimate=pl.CostEstimate(flops=0, bytes_accessed=5 * 10**6, transcendentals=0),
        name="query_grad_placed",
    )(pieces)


def join_kernel(wide, *refs):
    keep = refs[:2]
    both = refs[2 : 2 + wide]
    out = refs[-1]
    rest = refs[2 + wide : -1]
    count = len(rest) // 2
    slab, width = out.shape[0], out.shape[1] // 2
    for kind in range(2):
        at = slice(kind * width, (kind + 1) * width)
        total = keep[kind][:slab, :]
        for ref in both:
            total = total + ref[:, at].astype(F32)
        for ref in rest[kind * count : (kind + 1) * count]:
            total = total + ref[...].astype(F32)
        out[:, at] = total


def joined(slab, keep, both, rest):
    vmem = pl.BlockSpec(memory_space=pltpu.VMEM)
    return pl.pallas_call(
        lambda *refs: join_kernel(len(both), *refs),
        out_shape=jax.ShapeDtypeStruct((slab, 2 * keep[0].shape[1]), F32),
        in_specs=[vmem] * (2 + len(both) + len(rest)),
        out_specs=vmem,
        compiler_params=pltpu.CompilerParams(vmem_limit_bytes=ALL_VMEM_BYTES),
        cost_estimate=pl.CostEstimate(flops=0, bytes_accessed=3 * 10**6, transcendentals=0),
        name="weight_grad_joined",
    )(*keep, *both, *rest)


def local(layer_input, queries, key_states, value_states, out_grad):
    rows = layer_input.shape[0]
    cycle = lax.axis_size("seq")
    replicas = lax.axis_size("dp")
    groups = cycle // KVH
    halves = replicas // 2
    slab = D // (replicas * cycle)
    after = lax.optimization_barrier
    within = [[i + k for k in range(KVH)] for i in range(0, cycle, KVH)]

    def swap(array, k):
        return lax.ppermute(array, "seq", [(i, i ^ k) for i in range(cycle)])

    def across_cores(array):
        return lax.ppermute(array, "dp", [(i, i ^ 1) for i in range(replicas)])

    def exchange(array, parts=None):
        return lax.all_to_all(
            array, "seq", split_axis=0, concat_axis=0, tiled=True, axis_index_groups=parts
        )

    keys_values, sends, columns = packed(
        rows,
        groups,
        replicas * groups,
        slab,
        queries,
        out_grad,
        key_states,
        value_states,
        layer_input,
    )
    keys_values = exchange(keys_values)
    pieces = [swap(sends[k - 1], k) for k in range(1, KVH)]

    columns, pieces = after((columns, pieces))
    inputs = [columns[0]] + [swap(columns[k], k) for k in range(1, KVH - 1)]

    grads, own, down = attention(rows, groups, queries, out_grad, keys_values, pieces)
    last, inputs, down = after((columns[KVH - 1], inputs, down))
    inputs.append(swap(last, KVH - 1))

    received = [
        lax.ppermute(
            down[step - 1], "seq", [(i + step * KVH, i) for i in range(cycle - step * KVH)]
        )
        for step in range(1, groups)
    ]
    received, inputs = after((received, inputs))
    gathered = [None, None]
    others = [None, None]
    for kind in (1, 0):
        total = own[kind]
        for part in received:
            total = total + part[kind].astype(F32)
        total = total.astype(BF16)
        gathered[kind] = [total] + [swap(total, k) for k in range(1, KVH)]
        others[kind] = across_cores(jnp.concatenate(gathered[kind], axis=1))
    xt, xt_give = transposed(rows, halves, groups * slab, inputs)
    xt_other = across_cores(xt_give)

    narrow = [None, None]
    keep = [None, None]
    send = [None, None]
    keep[1], send[1], narrow[1] = weight_terms(
        rows, halves, groups, slab, gathered[1], others[1], xt, xt_other
    )

    def over_sequences(array):
        return [
            lax.ppermute(
                array[(apart - 1) * slab : apart * slab],
                "dp",
                [(i, i ^ (2 * apart)) for i in range(replicas)],
            )
            for apart in range(1, halves)
        ]

    first = [over_sequences(send[1][step]) for step in range(1, groups)]
    first, grads, others[0] = after((first, grads, others[0]))
    keep[0], send[0], narrow[0] = weight_terms(
        rows, halves, groups, slab, gathered[0], others[0], xt, xt_other, send[1][0]
    )
    second = [over_sequences(send[0][step]) for step in range(1, groups)]
    rest = []
    for kind, parts in ((0, second), (1, first)):
        for step in range(1, groups):
            total = keep[kind][step * slab : (step + 1) * slab]
            for part in parts[step - 1]:
                total = total + part.astype(F32)
            rest.append(swap(total.astype(BF16), step * KVH))
    weight_grad = joined(slab, keep, over_sequences(send[0][0]), rest)

    returned = exchange(grads.reshape(KVH, rows, WIDE), within)
    query_grad = placed(rows, returned)
    return (query_grad, narrow[0], narrow[1], weight_grad)


def solution(mesh):
    spec = P(("dp", "seq"), None)
    return jax.shard_map(
        local, mesh=mesh, in_specs=(spec,) * 5, out_specs=(spec,) * 4, check_vma=False
    )
```

```python
import math

import jax
import jax.numpy as jnp
from jax import lax
from jax.experimental import pallas as pl
from jax.experimental.pallas import tpu as pltpu
from jax.sharding import PartitionSpec as P

D = 8192
QH = 32
KVH = 4
HD = 128
GROUP = QH // KVH
WIDE = GROUP * HD
TILE = 256
NEGATIVE = -1e30
BF16 = jnp.bfloat16
F32 = jnp.float32
VMEM_BYTES = 24 * 1024 * 1024
ALL_VMEM_BYTES = 62 * 1024 * 1024

NT = (((1,), (1,)), ((), ()))


def pack_kernel(rows, groups, halves, *refs):
    q_hbm, do_hbm, k_hbm, v_hbm, x_hbm, kv_out = refs[:6]
    piece_out = refs[6 : 5 + KVH]
    give_out, kv_s, piece_s, give_s, sems, out_sems = refs[5 + KVH :]
    head = lax.axis_index("seq") % KVH
    core = lax.axis_index("dp") % 2
    width = give_s.shape[1] // halves

    def of(index, block):
        return pl.ds(pl.multiple_of(index * block, block), block)

    loads = []

    def load(copies):
        made = []
        for source, target in copies:
            made.append(pltpu.make_async_copy(source, target, sems.at[len(loads)]))
            made[-1].start()
            loads.append(made[-1])
        return made

    small = load(
        (
            array.at[:, k * HD : (k + 1) * HD],
            kv_s.at[group * KVH + k, :, kind * HD : (kind + 1) * HD],
        )
        for k in range(KVH)
        for group in range(groups)
        for kind, array in enumerate((k_hbm, v_hbm))
    )
    large = [
        load(
            (
                array.at[:, of(head ^ k, WIDE)],
                piece_s.at[k - 1, :, kind * WIDE : (kind + 1) * WIDE],
            )
            for kind, array in enumerate((q_hbm, do_hbm))
        )
        for k in range(1, KVH)
    ]
    give = load(
        (
            x_hbm.at[:, of(2 * half + 1 - core, width)],
            give_s.at[:, half * width : (half + 1) * width],
        )
        for half in range(halves)
    )
    outs = []

    def pass_on(copies, source, target):
        for copy in copies:
            copy.wait()
        outs.append(pltpu.make_async_copy(source, target, out_sems.at[len(outs)]))
        outs[-1].start()

    pass_on(small, kv_s, kv_out)
    for k in range(1, KVH):
        pass_on(large[k - 1], piece_s.at[k - 1], piece_out[k - 1])
    pass_on(give, give_s, give_out)
    for copy in outs:
        copy.wait()


def packed(rows, groups, halves, queries, out_grad, key_states, value_states, layer_input):
    any_spec = pl.BlockSpec(memory_space=pltpu.HBM)
    cycle = KVH * groups
    outs = pl.pallas_call(
        lambda *refs: pack_kernel(rows, groups, halves, *refs),
        out_shape=[jax.ShapeDtypeStruct((cycle, rows, 2 * HD), BF16)]
        + [jax.ShapeDtypeStruct((rows, 2 * WIDE), BF16)] * (KVH - 1)
        + [jax.ShapeDtypeStruct((rows, D // 2), BF16)],
        in_specs=[any_spec] * 5,
        out_specs=[any_spec] * (KVH + 1),
        scratch_shapes=[
            pltpu.VMEM((cycle, rows, 2 * HD), BF16),
            pltpu.VMEM((KVH - 1, rows, 2 * WIDE), BF16),
            pltpu.VMEM((rows, D // 2), BF16),
            pltpu.SemaphoreType.DMA((2 * cycle + 2 * KVH + halves,)),
            pltpu.SemaphoreType.DMA((KVH + 1,)),
        ],
        compiler_params=pltpu.CompilerParams(vmem_limit_bytes=ALL_VMEM_BYTES),
        cost_estimate=pl.CostEstimate(flops=0, bytes_accessed=8 * 10**6, transcendentals=0),
        name="first_sends",
    )(queries, out_grad, key_states, value_states, layer_input)
    return outs[0], outs[1:KVH], outs[KVH]


def column_blocks(halves, groups, k):
    place = lax.axis_index("seq")
    group = place // KVH
    head = place % KVH
    half = lax.axis_index("dp") // 2
    core = lax.axis_index("dp") % 2
    blocks = []
    for apart in range(halves):
        for step in range(groups):
            mine = (((half ^ apart) * 2 + core) * groups + (group ^ step)) * KVH + (head ^ k)
            given = ((half ^ apart) * groups + (group ^ step)) * KVH + (head ^ k)
            blocks.append((mine, given))
    return blocks


def column_kernel(rows, halves, groups, slab, *refs):
    x_hbm, given_hbm = refs[:2]
    outs = refs[2 : 2 + KVH]
    x_s, sems, out_sems = refs[2 + KVH :]
    loads = []
    for k in range(KVH):
        for b, places in enumerate(column_blocks(halves, groups, k)):
            for which, source in enumerate((x_hbm, given_hbm)):
                loads.append(
                    pltpu.make_async_copy(
                        source.at[:, pl.ds(pl.multiple_of(places[which] * slab, slab), slab)],
                        x_s.at[k, which * rows : (which + 1) * rows, b * slab : (b + 1) * slab],
                        sems.at[len(loads)],
                    )
                )
    for load in loads:
        load.start()
    stores = []
    each = len(loads) // KVH
    for k in range(KVH):
        for load in loads[k * each : (k + 1) * each]:
            load.wait()
        stores.append(pltpu.make_async_copy(x_s.at[k], outs[k], out_sems.at[k]))
        stores[-1].start()
    for store in stores:
        store.wait()


def columns_for_group(rows, halves, groups, slab, layer_input, given):
    width = halves * groups * slab
    if slab % HD:
        return [
            jnp.concatenate(
                [
                    jnp.concatenate(
                        [
                            lax.dynamic_slice_in_dim(array, places[which] * slab, slab, 1)
                            for places in column_blocks(halves, groups, k)
                        ],
                        axis=1,
                    )
                    for which, array in enumerate((layer_input, given))
                ],
                axis=0,
            )
            for k in range(KVH)
        ]
    any_spec = pl.BlockSpec(memory_space=pltpu.HBM)
    return pl.pallas_call(
        lambda *refs: column_kernel(rows, halves, groups, slab, *refs),
        out_shape=[jax.ShapeDtypeStruct((2 * rows, width), BF16)] * KVH,
        in_specs=[any_spec] * 2,
        out_specs=[any_spec] * KVH,
        scratch_shapes=[
            pltpu.VMEM((KVH, 2 * rows, width), BF16),
            pltpu.SemaphoreType.DMA((2 * KVH * halves * groups,)),
            pltpu.SemaphoreType.DMA((KVH,)),
        ],
        compiler_params=pltpu.CompilerParams(vmem_limit_bytes=ALL_VMEM_BYTES),
        cost_estimate=pl.CostEstimate(flops=0, bytes_accessed=8 * 10**6, transcendentals=0),
        name="input_columns",
    )(layer_input, given)


def attention_kernel(rows, groups, *refs):
    span = KVH * rows
    q_hbm, do_hbm, kv_hbm = refs[:3]
    pieces = refs[3 : 3 + KVH - 1]
    at = 3 + KVH - 1
    dq_out = refs[at]
    at += 1
    own_out = refs[at]
    at += 1
    down_out = refs[at : at + groups - 1]
    at += groups - 1
    q_s, do_s, k_s, v_s, kt_s, dk_s, dv_s, down_s, sems = refs[at:]

    place = lax.axis_index("seq")
    group = place // KVH
    head = place % KVH

    def row_at(k, base=0):
        return pl.ds(pl.multiple_of(base + (head ^ k) * rows, rows), rows)

    def column_at(block):
        return pl.ds(pl.multiple_of(head * block, block), block)

    copies = [
        pltpu.make_async_copy(q_hbm.at[:, column_at(WIDE)], q_s.at[row_at(0)], sems.at[0]),
        pltpu.make_async_copy(do_hbm.at[:, column_at(WIDE)], do_s.at[row_at(0)], sems.at[1]),
    ]
    for kind, target in enumerate((k_s, v_s)):
        copies += [
            pltpu.make_async_copy(
                kv_hbm.at[source, :, kind * HD : (kind + 1) * HD],
                target.at[source * rows : (source + 1) * rows],
                sems.at[2 * KVH + 2 * source + kind],
            )
            for source in range(KVH * groups)
        ]
    for k in range(1, KVH):
        piece = pieces[k - 1]
        copies += [
            pltpu.make_async_copy(piece.at[:, :WIDE], q_s.at[row_at(k)], sems.at[2 * k]),
            pltpu.make_async_copy(piece.at[:, WIDE:], do_s.at[row_at(k)], sems.at[2 * k + 1]),
        ]
    for copy in copies:
        copy.start()
    for copy in copies:
        copy.wait()

    dk_s[...] = jnp.zeros_like(dk_s)
    dv_s[...] = jnp.zeros_like(dv_s)
    scale = 1.0 / math.sqrt(HD)
    fold = scale * math.log2(math.e)

    for which in range(groups):

        @pl.when(group == which)
        def _(which=which):
            for block in range((which + 1) * span // TILE):
                keys = slice(block * TILE, (block + 1) * TILE)
                kt_s[:, keys] = k_s[keys, :].T

            def one_head(h, carry):
                columns = pl.ds(pl.multiple_of(h * HD, HD), HD)
                for part in range(span // TILE):
                    q = q_s[part * TILE : (part + 1) * TILE, columns]
                    do = do_s[part * TILE : (part + 1) * TILE, columns]
                    length = which * span + (part + 1) * TILE
                    blocks = length // TILE
                    scores = []
                    grads = []
                    for b in range(blocks):
                        keys = slice(b * TILE, (b + 1) * TILE)
                        one = lax.dot_general(k_s[keys, :], q, NT, preferred_element_type=F32)
                        if b == blocks - 1:
                            key_place = lax.broadcasted_iota(jnp.int32, (TILE, TILE), 0)
                            query_place = lax.broadcasted_iota(jnp.int32, (TILE, TILE), 1)
                            one = jnp.where(key_place <= query_place, one, NEGATIVE)
                        scores.append(one)
                        grads.append(
                            lax.dot_general(v_s[keys, :], do, NT, preferred_element_type=F32)
                        )
                    top = scores[0].max(axis=0, keepdims=True)
                    for one in scores[1:]:
                        top = jnp.maximum(top, one.max(axis=0, keepdims=True))
                    expon = [jnp.exp2((one - top) * fold) for one in scores]
                    denom = sum(e.sum(axis=0, keepdims=True) for e in expon)
                    weighted = sum(
                        (e * gp).sum(axis=0, keepdims=True) for e, gp in zip(expon, grads)
                    )
                    inverse = 1.0 / denom
                    delta = weighted * inverse
                    probs = jnp.concatenate([(e * inverse).astype(BF16) for e in expon], axis=0)
                    grad_scores = jnp.concatenate(
                        [
                            (e * (inverse * scale) * (gp - delta)).astype(BF16)
                            for e, gp in zip(expon, grads)
                        ],
                        axis=0,
                    )
                    dv_s[:length, :] += jnp.dot(probs, do, preferred_element_type=F32)
                    dk_s[:length, :] += jnp.dot(grad_scores, q, preferred_element_type=F32)
                    dqt = jnp.dot(kt_s[:, :length], grad_scores, preferred_element_type=F32)
                    dq_out[part * TILE : (part + 1) * TILE, columns] = dqt.T.astype(BF16)
                return carry

            lax.fori_loop(0, GROUP, one_head, 0)
            base = which * span
            own_out[:, :HD] = dk_s[base : base + span, :]
            own_out[:, HD:] = dv_s[base : base + span, :]
            for step in range(1, which + 1):
                source = (which - step) * span
                down_s[step - 1, :, :HD] = dk_s[source : source + span, :].astype(BF16)
                down_s[step - 1, :, HD:] = dv_s[source : source + span, :].astype(BF16)
            for step in range(which + 1, groups):
                down_s[step - 1] = jnp.zeros((span, 2 * HD), BF16)

    outs = [
        pltpu.make_async_copy(down_s.at[step], down_out[step], sems.at[step])
        for step in range(groups - 1)
    ]
    for copy in outs:
        copy.start()
    for copy in outs:
        copy.wait()


def attention(rows, groups, queries, out_grad, keys_values, pieces):
    span = KVH * rows
    length = groups * span
    any_spec = pl.BlockSpec(memory_space=pltpu.HBM)
    n_in = 3 + len(pieces)
    out_shape = (
        [jax.ShapeDtypeStruct((span, WIDE), BF16)]
        + [jax.ShapeDtypeStruct((span, 2 * HD), F32)]
        + [jax.ShapeDtypeStruct((span, 2 * HD), BF16)] * (groups - 1)
    )
    out_specs = (
        [pl.BlockSpec(memory_space=pltpu.VMEM)] * 2
        + [any_spec] * (groups - 1)
    )
    outs = pl.pallas_call(
        lambda *refs: attention_kernel(rows, groups, *refs),
        out_shape=out_shape,
        in_specs=[any_spec] * n_in,
        out_specs=out_specs,
        scratch_shapes=[
            pltpu.VMEM((span, WIDE), BF16),
            pltpu.VMEM((span, WIDE), BF16),
            pltpu.VMEM((length, HD), BF16),
            pltpu.VMEM((length, HD), BF16),
            pltpu.VMEM((HD, length), BF16),
            pltpu.VMEM((length, HD), F32),
            pltpu.VMEM((length, HD), F32),
            pltpu.VMEM((max(groups - 1, 1), span, 2 * HD), BF16),
            pltpu.SemaphoreType.DMA((2 * KVH + 2 * KVH * groups,)),
        ],
        compiler_params=pltpu.CompilerParams(vmem_limit_bytes=ALL_VMEM_BYTES),
        cost_estimate=pl.CostEstimate(flops=10**10, bytes_accessed=5 * 10**7, transcendentals=0),
        name="attention",
    )(queries, out_grad, keys_values, *pieces)
    return outs[0], outs[1], outs[2:]


def weight_kernel(rows, halves, groups, slab, *refs):
    own = refs[:KVH]
    other = refs[KVH : 2 * KVH]
    x = refs[2 * KVH : 3 * KVH]
    keep, same = refs[3 * KVH : 3 * KVH + 2]
    at = 3 * KVH + 2
    away = (refs[at : at + groups - 1], refs[at + groups - 1 : at + 2 * groups - 2])
    mine_out = refs[at + 2 * groups - 2 : at + 2 * groups]
    g_s = refs[-1]
    width = KVH * HD
    head = lax.axis_index("seq") % KVH
    mine = pl.ds(pl.multiple_of(head * rows, rows), rows)
    for k in range(KVH):
        for kind in range(2):
            part = slice(kind * HD, (kind + 1) * HD)
            columns = pl.ds(pl.multiple_of((head ^ k) * HD, HD), HD)
            wide = pl.ds(pl.multiple_of(kind * width + (head ^ k) * HD, HD), HD)
            mine_out[kind][:, columns] = own[k][mine, part]
            for far in range(KVH):
                lines = pl.ds(pl.multiple_of((head ^ far) * rows, rows), rows)
                first = 2 * far * rows
                g_s[first : first + rows, wide] = own[k][lines, part]
                g_s[first + rows : first + 2 * rows, wide] = other[k][lines, part]
    for apart in range(halves - 1, -1, -1):
        for step in range(groups - 1, -1, -1):
            block = (apart * groups + step) * slab
            left = jnp.concatenate([x[k][:, block : block + slab].T for k in range(KVH)], axis=1)
            product = jnp.dot(left, g_s[...], preferred_element_type=F32)
            lines = slice((apart - 1) * slab, apart * slab)
            if apart == 0:
                keep[step * slab : (step + 1) * slab, :] = product
            elif step == 0:
                same[lines, :] = product.astype(BF16)
            else:
                for kind in range(2):
                    away[kind][step - 1][lines, :] = product[
                        :, kind * width : (kind + 1) * width
                    ].astype(BF16)


def weight_terms(rows, halves, groups, slab, own, other, inputs):
    span = KVH * rows
    channels = KVH * HD
    vmem = pl.BlockSpec(memory_space=pltpu.VMEM)
    others = max(halves - 1, 1) * slab
    outs = pl.pallas_call(
        lambda *refs: weight_kernel(rows, halves, groups, slab, *refs),
        out_shape=[
            jax.ShapeDtypeStruct((groups * slab, 2 * channels), F32),
            jax.ShapeDtypeStruct((others, 2 * channels), BF16),
        ]
        + [jax.ShapeDtypeStruct((others, channels), BF16)] * (2 * (groups - 1))
        + [jax.ShapeDtypeStruct((rows, channels), BF16)] * 2,
        in_specs=[vmem] * (3 * KVH),
        out_specs=[vmem] * (2 * groups + 2),
        scratch_shapes=[pltpu.VMEM((2 * span, 2 * channels), BF16)],
        compiler_params=pltpu.CompilerParams(vmem_limit_bytes=VMEM_BYTES),
        cost_estimate=pl.CostEstimate(flops=3 * 10**9, bytes_accessed=6 * 10**6, transcendentals=0),
        name="weight_terms",
    )(*own, *other, *inputs)
    at = groups - 1
    away = outs[2 : 2 + 2 * at]
    return outs[0], outs[1], (away[:at], away[at:]), outs[2 + 2 * at :]


def place_kernel(pieces, out):
    for head in range(KVH):
        out[:, head * WIDE : (head + 1) * WIDE] = pieces[head]


def placed(rows, pieces):
    vmem = pl.BlockSpec(memory_space=pltpu.VMEM)
    return pl.pallas_call(
        place_kernel,
        out_shape=jax.ShapeDtypeStruct((rows, QH * HD), BF16),
        in_specs=[vmem],
        out_specs=vmem,
        compiler_params=pltpu.CompilerParams(vmem_limit_bytes=VMEM_BYTES),
        cost_estimate=pl.CostEstimate(flops=0, bytes_accessed=5 * 10**6, transcendentals=0),
        name="query_grad_placed",
    )(pieces)


def add_kernel(kind, step, keep, *refs):
    out = refs[-1]
    slab, width = out.shape
    total = keep[step * slab : (step + 1) * slab, kind * width : (kind + 1) * width]
    for ref in refs[:-1]:
        total = total + ref[...].astype(F32)
    out[...] = total.astype(BF16)


def added(keep, parts, kind, step):
    vmem = pl.BlockSpec(memory_space=pltpu.VMEM)
    return pl.pallas_call(
        lambda *refs: add_kernel(kind, step, *refs),
        out_shape=jax.ShapeDtypeStruct(parts[0].shape, BF16),
        in_specs=[vmem] * (1 + len(parts)),
        out_specs=vmem,
        compiler_params=pltpu.CompilerParams(vmem_limit_bytes=VMEM_BYTES),
        cost_estimate=pl.CostEstimate(flops=0, bytes_accessed=10**6, transcendentals=0),
        name="sequences_added",
    )(keep, *parts)


def join_kernel(wide, *refs):
    keep = refs[0]
    both = refs[1 : 1 + wide]
    out = refs[-1]
    rest = refs[1 + wide : -1]
    count = len(rest) // 2
    slab, width = out.shape[0], out.shape[1] // 2
    for kind in range(2):
        at = slice(kind * width, (kind + 1) * width)
        total = keep[:slab, at]
        for ref in both:
            total = total + ref[:, at].astype(F32)
        for ref in rest[kind * count : (kind + 1) * count]:
            total = total + ref[...].astype(F32)
        out[:, at] = total


def joined(slab, keep, both, rest):
    vmem = pl.BlockSpec(memory_space=pltpu.VMEM)
    return pl.pallas_call(
        lambda *refs: join_kernel(len(both), *refs),
        out_shape=jax.ShapeDtypeStruct((slab, keep.shape[1]), F32),
        in_specs=[vmem] * (1 + len(both) + len(rest)),
        out_specs=vmem,
        compiler_params=pltpu.CompilerParams(vmem_limit_bytes=VMEM_BYTES),
        cost_estimate=pl.CostEstimate(flops=0, bytes_accessed=3 * 10**6, transcendentals=0),
        name="weight_grad_joined",
    )(keep, *both, *rest)


def local(layer_input, queries, key_states, value_states, out_grad):
    rows = layer_input.shape[0]
    cycle = lax.axis_size("seq")
    replicas = lax.axis_size("dp")
    groups = cycle // KVH
    halves = replicas // 2
    slab = D // (replicas * cycle)
    after = lax.optimization_barrier
    within = [[i + k for k in range(KVH)] for i in range(0, cycle, KVH)]

    def swap(array, k):
        return lax.ppermute(array, "seq", [(i, i ^ k) for i in range(cycle)])

    def across_cores(array):
        return lax.ppermute(array, "dp", [(i, i ^ 1) for i in range(replicas)])

    def exchange(array, parts=None):
        return lax.all_to_all(
            array, "seq", split_axis=0, concat_axis=0, tiled=True, axis_index_groups=parts
        )

    keys_values, sends, give = packed(
        rows, groups, halves, queries, out_grad, key_states, value_states, layer_input
    )
    keys_values = exchange(keys_values)
    pieces = [None] * KVH
    for k in range(KVH - 1, 0, -1):
        pieces[k] = swap(sends[k - 1], k)
    pieces = pieces[1:]

    columns = columns_for_group(rows, halves, groups, slab, layer_input, across_cores(give))
    columns, pieces = after((columns, pieces))
    inputs = [columns[0], None] + [swap(columns[k], k) for k in range(2, KVH)]

    grads, own, down = attention(rows, groups, queries, out_grad, keys_values, pieces)
    columns, inputs[2:], down = after((columns, inputs[2:], down))
    inputs[1] = swap(columns[1], 1)

    received = [
        lax.ppermute(
            down[step - 1], "seq", [(i + step * KVH, i) for i in range(cycle - step * KVH)]
        )
        for step in range(1, groups)
    ]
    received, inputs[1] = after((received, inputs[1]))
    total = own
    for part in received:
        total = total + part.astype(F32)
    total = total.astype(BF16)
    gathered = [total] + [swap(total, k) for k in range(1, KVH)]
    others = [across_cores(piece) for piece in gathered]
    keep, same, away, narrow = weight_terms(
        rows, halves, groups, slab, gathered, others, inputs
    )

    def over_sequences(array):
        return [
            lax.ppermute(
                array[(apart - 1) * slab : apart * slab],
                "dp",
                [(i, i ^ (2 * apart)) for i in range(replicas)],
            )
            for apart in range(1, halves)
        ]

    parts = [[over_sequences(array) for array in away[kind]] for kind in range(2)]
    rest = [[], []]
    for kind in (1, 0):
        totals = [
            added(keep, parts[kind][step - 1], kind, step) for step in range(1, groups)
        ]
        rest[kind] = [swap(total, (step + 1) * KVH) for step, total in enumerate(totals)]
    weight_grad = joined(slab, keep, over_sequences(same), rest[0] + rest[1])

    returned = exchange(grads.reshape(KVH, rows, WIDE), within)
    query_grad = placed(rows, returned)
    return (query_grad, narrow[0], narrow[1], weight_grad)


def solution(mesh):
    spec = P(("dp", "seq"), None)
    return jax.shard_map(
        local, mesh=mesh, in_specs=(spec,) * 5, out_specs=(spec,) * 4, check_vma=False
    )
```

```python
import math

import jax
import jax.numpy as jnp
from jax import lax
from jax.experimental import pallas as pl
from jax.experimental.pallas import tpu as pltpu
from jax.sharding import PartitionSpec as P

D = 8192
QH = 32
KVH = 4
HD = 128
GROUP = QH // KVH
WIDE = GROUP * HD
TILE = 256
PART = 4 * HD
NEGATIVE = -1e30
BF16 = jnp.bfloat16
F32 = jnp.float32
VMEM_BYTES = 24 * 1024 * 1024
ALL_VMEM_BYTES = 62 * 1024 * 1024

NT = (((1,), (1,)), ((), ()))


def pack_kernel(rows, groups, halves, *refs):
    q_hbm, do_hbm, k_hbm, v_hbm, x_hbm, kv_out = refs[:6]
    piece_out = refs[6 : 5 + KVH]
    give_out, kv_s, piece_s, give_s, sems, out_sems = refs[5 + KVH :]
    head = lax.axis_index("seq") % KVH
    core = lax.axis_index("dp") % 2
    width = give_s.shape[1] // halves

    def of(index, block):
        return pl.ds(pl.multiple_of(index * block, block), block)

    loads = []

    def load(copies):
        made = []
        for source, target in copies:
            made.append(pltpu.make_async_copy(source, target, sems.at[len(loads)]))
            made[-1].start()
            loads.append(made[-1])
        return made

    small = load(
        (
            array.at[:, k * HD : (k + 1) * HD],
            kv_s.at[group * KVH + k, :, kind * HD : (kind + 1) * HD],
        )
        for k in range(KVH)
        for group in range(groups)
        for kind, array in enumerate((k_hbm, v_hbm))
    )
    large = [
        load(
            (
                array.at[:, of(head ^ k, WIDE)],
                piece_s.at[k - 1, :, kind * WIDE : (kind + 1) * WIDE],
            )
            for kind, array in enumerate((q_hbm, do_hbm))
        )
        for k in range(1, KVH)
    ]
    give = load(
        (
            x_hbm.at[:, of(2 * half + 1 - core, width)],
            give_s.at[:, half * width : (half + 1) * width],
        )
        for half in range(halves)
    )
    outs = []

    def pass_on(copies, source, target):
        for copy in copies:
            copy.wait()
        outs.append(pltpu.make_async_copy(source, target, out_sems.at[len(outs)]))
        outs[-1].start()

    pass_on(small, kv_s, kv_out)
    for k in range(1, KVH):
        pass_on(large[k - 1], piece_s.at[k - 1], piece_out[k - 1])
    pass_on(give, give_s, give_out)
    for copy in outs:
        copy.wait()


def packed(rows, groups, halves, queries, out_grad, key_states, value_states, layer_input):
    any_spec = pl.BlockSpec(memory_space=pltpu.HBM)
    cycle = KVH * groups
    outs = pl.pallas_call(
        lambda *refs: pack_kernel(rows, groups, halves, *refs),
        out_shape=[jax.ShapeDtypeStruct((cycle, rows, 2 * HD), BF16)]
        + [jax.ShapeDtypeStruct((rows, 2 * WIDE), BF16)] * (KVH - 1)
        + [jax.ShapeDtypeStruct((rows, D // 2), BF16)],
        in_specs=[any_spec] * 5,
        out_specs=[any_spec] * (KVH + 1),
        scratch_shapes=[
            pltpu.VMEM((cycle, rows, 2 * HD), BF16),
            pltpu.VMEM((KVH - 1, rows, 2 * WIDE), BF16),
            pltpu.VMEM((rows, D // 2), BF16),
            pltpu.SemaphoreType.DMA((2 * cycle + 2 * KVH + halves,)),
            pltpu.SemaphoreType.DMA((KVH + 1,)),
        ],
        compiler_params=pltpu.CompilerParams(vmem_limit_bytes=ALL_VMEM_BYTES),
        cost_estimate=pl.CostEstimate(flops=0, bytes_accessed=8 * 10**6, transcendentals=0),
        name="first_sends",
    )(queries, out_grad, key_states, value_states, layer_input)
    return outs[0], outs[1:KVH], outs[KVH]


def column_blocks(halves, groups, k):
    place = lax.axis_index("seq")
    group = place // KVH
    head = place % KVH
    half = lax.axis_index("dp") // 2
    core = lax.axis_index("dp") % 2
    blocks = []
    for apart in range(halves):
        for step in range(groups):
            mine = (((half ^ apart) * 2 + core) * groups + (group ^ step)) * KVH + (head ^ k)
            given = ((half ^ apart) * groups + (group ^ step)) * KVH + (head ^ k)
            blocks.append((mine, given))
    return blocks


def column_kernel(rows, halves, groups, slab, *refs):
    x_hbm, given_hbm = refs[:2]
    outs = refs[2 : 2 + KVH]
    x_s, sems, out_sems = refs[2 + KVH :]
    loads = []
    for k in range(KVH):
        for b, places in enumerate(column_blocks(halves, groups, k)):
            for which, source in enumerate((x_hbm, given_hbm)):
                loads.append(
                    pltpu.make_async_copy(
                        source.at[:, pl.ds(pl.multiple_of(places[which] * slab, slab), slab)],
                        x_s.at[k, which * rows : (which + 1) * rows, b * slab : (b + 1) * slab],
                        sems.at[len(loads)],
                    )
                )
    for load in loads:
        load.start()
    stores = []
    each = len(loads) // KVH
    for k in range(KVH):
        for load in loads[k * each : (k + 1) * each]:
            load.wait()
        stores.append(pltpu.make_async_copy(x_s.at[k], outs[k], out_sems.at[k]))
        stores[-1].start()
    for store in stores:
        store.wait()


def columns_for_group(rows, halves, groups, slab, layer_input, given):
    width = halves * groups * slab
    if slab % HD:
        return [
            jnp.concatenate(
                [
                    jnp.concatenate(
                        [
                            lax.dynamic_slice_in_dim(array, places[which] * slab, slab, 1)
                            for places in column_blocks(halves, groups, k)
                        ],
                        axis=1,
                    )
                    for which, array in enumerate((layer_input, given))
                ],
                axis=0,
            )
            for k in range(KVH)
        ]
    any_spec = pl.BlockSpec(memory_space=pltpu.HBM)
    return pl.pallas_call(
        lambda *refs: column_kernel(rows, halves, groups, slab, *refs),
        out_shape=[jax.ShapeDtypeStruct((2 * rows, width), BF16)] * KVH,
        in_specs=[any_spec] * 2,
        out_specs=[any_spec] * KVH,
        scratch_shapes=[
            pltpu.VMEM((KVH, 2 * rows, width), BF16),
            pltpu.SemaphoreType.DMA((2 * KVH * halves * groups,)),
            pltpu.SemaphoreType.DMA((KVH,)),
        ],
        compiler_params=pltpu.CompilerParams(vmem_limit_bytes=ALL_VMEM_BYTES),
        cost_estimate=pl.CostEstimate(flops=0, bytes_accessed=8 * 10**6, transcendentals=0),
        name="input_columns",
    )(layer_input, given)


def attention_kernel(rows, groups, *refs):
    span = KVH * rows
    q_hbm, do_hbm, kv_hbm = refs[:3]
    pieces = refs[3 : 3 + KVH - 1]
    at = 3 + KVH - 1
    dq_out = refs[at : at + KVH]
    at += KVH
    own_out = refs[at]
    at += 1
    down_out = refs[at : at + groups - 1]
    at += groups - 1
    q_s, do_s, dq_s, k_s, v_s, kt_s, dk_s, dv_s, down_s, sems, q_sems, dq_sems = refs[at:]

    place = lax.axis_index("seq")
    group = place // KVH
    head = place % KVH

    def row_at(k, base=0):
        return pl.ds(pl.multiple_of(base + (head ^ k) * rows, rows), rows)

    def column_at(block):
        return pl.ds(pl.multiple_of(head * block, block), block)

    def loads(chunk):
        first = chunk * PART
        made = []
        for k in range(KVH):
            for kind, target in enumerate((q_s, do_s)):
                if k:
                    source = pieces[k - 1].at[:, pl.ds(pl.multiple_of(kind * WIDE + first, PART), PART)]
                else:
                    source = (q_hbm, do_hbm)[kind].at[
                        :, pl.ds(pl.multiple_of(head * WIDE + first, PART), PART)
                    ]
                made.append(
                    pltpu.make_async_copy(
                        source,
                        target.at[row_at(k), pl.ds(pl.multiple_of(first, PART), PART)],
                        q_sems.at[chunk, 2 * k + kind],
                    )
                )
        return made

    def stores(chunk):
        columns = pl.ds(pl.multiple_of(chunk * PART, PART), PART)
        return [
            pltpu.make_async_copy(
                dq_s.at[row_at(k), columns], dq_out[k].at[:, columns], dq_sems.at[chunk, k]
            )
            for k in range(KVH)
        ]

    copies = []
    for kind, target in enumerate((k_s, v_s)):
        copies += [
            pltpu.make_async_copy(
                kv_hbm.at[source, :, kind * HD : (kind + 1) * HD],
                target.at[source * rows : (source + 1) * rows],
                sems.at[2 * source + kind],
            )
            for source in range(KVH * groups)
        ]
    for copy in copies + loads(0):
        copy.start()
    for chunk in range(1, WIDE // PART):
        for copy in loads(chunk):
            copy.start()
    for copy in copies:
        copy.wait()

    dk_s[...] = jnp.zeros_like(dk_s)
    dv_s[...] = jnp.zeros_like(dv_s)
    scale = 1.0 / math.sqrt(HD)
    fold = scale * math.log2(math.e)

    for which in range(groups):

        @pl.when(group == which)
        def _(which=which):
            for block in range((which + 1) * span // TILE):
                keys = slice(block * TILE, (block + 1) * TILE)
                kt_s[:, keys] = k_s[keys, :].T

            def one_head(h, carry):
                columns = pl.ds(pl.multiple_of(h * HD, HD), HD)
                for part in range(span // TILE):
                    q = q_s[part * TILE : (part + 1) * TILE, columns]
                    do = do_s[part * TILE : (part + 1) * TILE, columns]
                    length = which * span + (part + 1) * TILE
                    blocks = length // TILE
                    scores = []
                    grads = []
                    for b in range(blocks):
                        keys = slice(b * TILE, (b + 1) * TILE)
                        one = lax.dot_general(k_s[keys, :], q, NT, preferred_element_type=F32)
                        if b == blocks - 1:
                            key_place = lax.broadcasted_iota(jnp.int32, (TILE, TILE), 0)
                            query_place = lax.broadcasted_iota(jnp.int32, (TILE, TILE), 1)
                            one = jnp.where(key_place <= query_place, one, NEGATIVE)
                        scores.append(one)
                        grads.append(
                            lax.dot_general(v_s[keys, :], do, NT, preferred_element_type=F32)
                        )
                    top = scores[0].max(axis=0, keepdims=True)
                    for one in scores[1:]:
                        top = jnp.maximum(top, one.max(axis=0, keepdims=True))
                    expon = [jnp.exp2((one - top) * fold) for one in scores]
                    denom = sum(e.sum(axis=0, keepdims=True) for e in expon)
                    weighted = sum(
                        (e * gp).sum(axis=0, keepdims=True) for e, gp in zip(expon, grads)
                    )
                    inverse = 1.0 / denom
                    delta = weighted * inverse
                    probs = jnp.concatenate([(e * inverse).astype(BF16) for e in expon], axis=0)
                    grad_scores = jnp.concatenate(
                        [
                            (e * (inverse * scale) * (gp - delta)).astype(BF16)
                            for e, gp in zip(expon, grads)
                        ],
                        axis=0,
                    )
                    dv_s[:length, :] += jnp.dot(probs, do, preferred_element_type=F32)
                    dk_s[:length, :] += jnp.dot(grad_scores, q, preferred_element_type=F32)
                    dqt = jnp.dot(kt_s[:, :length], grad_scores, preferred_element_type=F32)
                    dq_s[part * TILE : (part + 1) * TILE, columns] = dqt.T.astype(BF16)
                return carry

            def one_chunk(chunk, carry):
                for copy in loads(chunk):
                    copy.wait()
                for h in range(PART // HD):
                    one_head(chunk * (PART // HD) + h, 0)
                for copy in stores(chunk):
                    copy.start()
                return carry

            lax.fori_loop(0, WIDE // PART, one_chunk, 0)
            base = which * span
            own_out[:, :HD] = dk_s[base : base + span, :]
            own_out[:, HD:] = dv_s[base : base + span, :]
            for step in range(1, which + 1):
                source = (which - step) * span
                down_s[step - 1, :, :HD] = dk_s[source : source + span, :].astype(BF16)
                down_s[step - 1, :, HD:] = dv_s[source : source + span, :].astype(BF16)
            for step in range(which + 1, groups):
                down_s[step - 1] = jnp.zeros((span, 2 * HD), BF16)

    outs = [
        pltpu.make_async_copy(down_s.at[step], down_out[step], sems.at[step])
        for step in range(groups - 1)
    ]
    for copy in outs:
        copy.start()
    for chunk in range(WIDE // PART):
        outs += stores(chunk)
    for copy in outs:
        copy.wait()


def attention(rows, groups, queries, out_grad, keys_values, pieces):
    span = KVH * rows
    length = groups * span
    any_spec = pl.BlockSpec(memory_space=pltpu.HBM)
    n_in = 3 + len(pieces)
    out_shape = (
        [jax.ShapeDtypeStruct((rows, WIDE), BF16)] * KVH
        + [jax.ShapeDtypeStruct((span, 2 * HD), F32)]
        + [jax.ShapeDtypeStruct((span, 2 * HD), BF16)] * (groups - 1)
    )
    out_specs = (
        [any_spec] * KVH
        + [pl.BlockSpec(memory_space=pltpu.VMEM)]
        + [any_spec] * (groups - 1)
    )
    outs = pl.pallas_call(
        lambda *refs: attention_kernel(rows, groups, *refs),
        out_shape=out_shape,
        in_specs=[any_spec] * n_in,
        out_specs=out_specs,
        scratch_shapes=[
            pltpu.VMEM((span, WIDE), BF16),
            pltpu.VMEM((span, WIDE), BF16),
            pltpu.VMEM((span, WIDE), BF16),
            pltpu.VMEM((length, HD), BF16),
            pltpu.VMEM((length, HD), BF16),
            pltpu.VMEM((HD, length), BF16),
            pltpu.VMEM((length, HD), F32),
            pltpu.VMEM((length, HD), F32),
            pltpu.VMEM((max(groups - 1, 1), span, 2 * HD), BF16),
            pltpu.SemaphoreType.DMA((2 * KVH * groups,)),
            pltpu.SemaphoreType.DMA((WIDE // PART, 2 * KVH)),
            pltpu.SemaphoreType.DMA((WIDE // PART, KVH)),
        ],
        compiler_params=pltpu.CompilerParams(vmem_limit_bytes=ALL_VMEM_BYTES),
        cost_estimate=pl.CostEstimate(flops=10**10, bytes_accessed=5 * 10**7, transcendentals=0),
        name="attention",
    )(queries, out_grad, keys_values, *pieces)
    return outs[:KVH], outs[KVH], outs[KVH + 1 :]


def products(x, g_s, block, slab):
    left = jnp.concatenate([x[k][:, block : block + slab].T for k in range(KVH)], axis=1)
    return jnp.dot(left, g_s[...], preferred_element_type=F32)


def away_kernel(rows, halves, groups, slab, *refs):
    own = refs[:KVH]
    other = refs[KVH : 2 * KVH]
    x = refs[2 * KVH : 3 * KVH]
    at = 3 * KVH
    away = (refs[at : at + groups - 1], refs[at + groups - 1 : at + 2 * groups - 2])
    mine_out = refs[at + 2 * groups - 2 : at + 2 * groups]
    g_s = refs[-1]
    width = KVH * HD
    head = lax.axis_index("seq") % KVH
    mine = pl.ds(pl.multiple_of(head * rows, rows), rows)
    for k in range(KVH):
        for kind in range(2):
            part = slice(kind * HD, (kind + 1) * HD)
            columns = pl.ds(pl.multiple_of((head ^ k) * HD, HD), HD)
            wide = pl.ds(pl.multiple_of(kind * width + (head ^ k) * HD, HD), HD)
            mine_out[kind][:, columns] = own[k][mine, part]
            for far in range(KVH):
                lines = pl.ds(pl.multiple_of((head ^ far) * rows, rows), rows)
                first = 2 * far * rows
                g_s[first : first + rows, wide] = own[k][lines, part]
                g_s[first + rows : first + 2 * rows, wide] = other[k][lines, part]
    for apart in range(1, halves):
        for step in range(1, groups):
            product = products(x, g_s, (apart * groups + step) * slab, slab)
            lines = slice((apart - 1) * slab, apart * slab)
            for kind in range(2):
                away[kind][step - 1][lines, :] = product[
                    :, kind * width : (kind + 1) * width
                ].astype(BF16)


def away_terms(rows, halves, groups, slab, own, other, inputs):
    span = KVH * rows
    channels = KVH * HD
    vmem = pl.BlockSpec(memory_space=pltpu.VMEM)
    others = max(halves - 1, 1) * slab
    outs = pl.pallas_call(
        lambda *refs: away_kernel(rows, halves, groups, slab, *refs),
        out_shape=[jax.ShapeDtypeStruct((others, channels), BF16)] * (2 * (groups - 1))
        + [jax.ShapeDtypeStruct((rows, channels), BF16)] * 2
        + [jax.ShapeDtypeStruct((2 * span, 2 * channels), BF16)],
        in_specs=[vmem] * (3 * KVH),
        out_specs=[vmem] * (2 * groups + 1),
        compiler_params=pltpu.CompilerParams(vmem_limit_bytes=VMEM_BYTES),
        cost_estimate=pl.CostEstimate(flops=10**9, bytes_accessed=6 * 10**6, transcendentals=0),
        name="weight_terms_away",
    )(*own, *other, *inputs)
    at = groups - 1
    return (outs[:at], outs[at : 2 * at]), outs[2 * at : 2 * at + 2], outs[-1]


def near_kernel(halves, groups, slab, *refs):
    x = refs[:KVH]
    g_s, keep, same = refs[KVH:]
    for step in range(groups - 1, -1, -1):
        keep[step * slab : (step + 1) * slab, :] = products(x, g_s, step * slab, slab)
    for apart in range(1, halves):
        product = products(x, g_s, apart * groups * slab, slab)
        same[(apart - 1) * slab : apart * slab, :] = product.astype(BF16)


def near_terms(halves, groups, slab, inputs, joined_grads):
    channels = joined_grads.shape[1]
    vmem = pl.BlockSpec(memory_space=pltpu.VMEM)
    return pl.pallas_call(
        lambda *refs: near_kernel(halves, groups, slab, *refs),
        out_shape=[
            jax.ShapeDtypeStruct((groups * slab, channels), F32),
            jax.ShapeDtypeStruct((max(halves - 1, 1) * slab, channels), BF16),
        ],
        in_specs=[vmem] * (KVH + 1),
        out_specs=[vmem] * 2,
        compiler_params=pltpu.CompilerParams(vmem_limit_bytes=VMEM_BYTES),
        cost_estimate=pl.CostEstimate(flops=2 * 10**9, bytes_accessed=6 * 10**6, transcendentals=0),
        name="weight_terms_near",
    )(*inputs, joined_grads)


def place_kernel(*refs):
    out = refs[KVH]
    head = lax.axis_index("seq") % KVH
    for k in range(KVH):
        out[:, pl.ds(pl.multiple_of((head ^ k) * WIDE, WIDE), WIDE)] = refs[k][...]


def placed(rows, pieces):
    vmem = pl.BlockSpec(memory_space=pltpu.VMEM)
    return pl.pallas_call(
        place_kernel,
        out_shape=jax.ShapeDtypeStruct((rows, QH * HD), BF16),
        in_specs=[vmem] * KVH,
        out_specs=vmem,
        compiler_params=pltpu.CompilerParams(vmem_limit_bytes=VMEM_BYTES),
        cost_estimate=pl.CostEstimate(flops=0, bytes_accessed=5 * 10**6, transcendentals=0),
        name="query_grad_placed",
    )(*pieces)


def add_kernel(kind, step, keep, *refs):
    out = refs[-1]
    slab, width = out.shape
    total = keep[step * slab : (step + 1) * slab, kind * width : (kind + 1) * width]
    for ref in refs[:-1]:
        total = total + ref[...].astype(F32)
    out[...] = total.astype(BF16)


def added(keep, parts, kind, step):
    vmem = pl.BlockSpec(memory_space=pltpu.VMEM)
    return pl.pallas_call(
        lambda *refs: add_kernel(kind, step, *refs),
        out_shape=jax.ShapeDtypeStruct(parts[0].shape, BF16),
        in_specs=[vmem] * (1 + len(parts)),
        out_specs=vmem,
        compiler_params=pltpu.CompilerParams(vmem_limit_bytes=VMEM_BYTES),
        cost_estimate=pl.CostEstimate(flops=0, bytes_accessed=10**6, transcendentals=0),
        name="sequences_added",
    )(keep, *parts)


def join_kernel(wide, *refs):
    keep = refs[0]
    both = refs[1 : 1 + wide]
    out = refs[-1]
    rest = refs[1 + wide : -1]
    count = len(rest) // 2
    slab, width = out.shape[0], out.shape[1] // 2
    for kind in range(2):
        at = slice(kind * width, (kind + 1) * width)
        total = keep[:slab, at]
        for ref in both:
            total = total + ref[:, at].astype(F32)
        for ref in rest[kind * count : (kind + 1) * count]:
            total = total + ref[...].astype(F32)
        out[:, at] = total


def joined(slab, keep, both, rest):
    vmem = pl.BlockSpec(memory_space=pltpu.VMEM)
    return pl.pallas_call(
        lambda *refs: join_kernel(len(both), *refs),
        out_shape=jax.ShapeDtypeStruct((slab, keep.shape[1]), F32),
        in_specs=[vmem] * (1 + len(both) + len(rest)),
        out_specs=vmem,
        compiler_params=pltpu.CompilerParams(vmem_limit_bytes=VMEM_BYTES),
        cost_estimate=pl.CostEstimate(flops=0, bytes_accessed=3 * 10**6, transcendentals=0),
        name="weight_grad_joined",
    )(keep, *both, *rest)


def local(layer_input, queries, key_states, value_states, out_grad):
    rows = layer_input.shape[0]
    cycle = lax.axis_size("seq")
    replicas = lax.axis_size("dp")
    groups = cycle // KVH
    halves = replicas // 2
    slab = D // (replicas * cycle)
    after = lax.optimization_barrier
    within = [[i + k for k in range(KVH)] for i in range(0, cycle, KVH)]

    def swap(array, k):
        return lax.ppermute(array, "seq", [(i, i ^ k) for i in range(cycle)])

    def across_cores(array):
        return lax.ppermute(array, "dp", [(i, i ^ 1) for i in range(replicas)])

    def exchange(array, parts=None):
        return lax.all_to_all(
            array, "seq", split_axis=0, concat_axis=0, tiled=True, axis_index_groups=parts
        )

    keys_values, sends, give = packed(
        rows, groups, halves, queries, out_grad, key_states, value_states, layer_input
    )
    keys_values = exchange(keys_values)
    pieces = [None] * KVH
    for k in range(KVH - 1, 0, -1):
        pieces[k] = swap(sends[k - 1], k)
    pieces = pieces[1:]

    columns = columns_for_group(rows, halves, groups, slab, layer_input, across_cores(give))
    columns, pieces = after((columns, pieces))
    inputs = [columns[0], None] + [swap(columns[k], k) for k in range(2, KVH)]

    grads, own, down = attention(rows, groups, queries, out_grad, keys_values, pieces)
    columns, inputs[2:], down = after((columns, inputs[2:], down))
    inputs[1] = swap(columns[1], 1)

    received = [
        lax.ppermute(
            down[step - 1], "seq", [(i + step * KVH, i) for i in range(cycle - step * KVH)]
        )
        for step in range(1, groups)
    ]
    received, inputs[1] = after((received, inputs[1]))
    total = own
    for part in received:
        total = total + part.astype(F32)
    total = total.astype(BF16)
    gathered = [total] + [swap(total, k) for k in range(1, KVH)]
    others = [across_cores(piece) for piece in gathered]
    away, narrow, joined_grads = away_terms(
        rows, halves, groups, slab, gathered, others, inputs
    )
    keep, same = near_terms(halves, groups, slab, inputs, joined_grads)

    def over_sequences(array):
        return [
            lax.ppermute(
                array[(apart - 1) * slab : apart * slab],
                "dp",
                [(i, i ^ (2 * apart)) for i in range(replicas)],
            )
            for apart in range(1, halves)
        ]

    parts = [[over_sequences(array) for array in away[kind]] for kind in range(2)]
    returned = [grads[0]] + [swap(grads[k], k) for k in range(1, KVH)]

    totals = [None, None]
    rest = [None, None]
    for kind in (1, 0):
        if not kind:
            parts[0], _ = after((parts[0], returned))
        totals[kind] = [
            added(keep, parts[kind][step - 1], kind, step) for step in range(1, groups)
        ]
        rest[kind] = [swap(total, (step + 1) * KVH) for step, total in enumerate(totals[kind])]
    weight_grad = joined(slab, keep, over_sequences(same), rest[0] + rest[1])
    query_grad = placed(rows, returned)
    return (query_grad, narrow[0], narrow[1], weight_grad)


def solution(mesh):
    spec = P(("dp", "seq"), None)
    return jax.shard_map(
        local, mesh=mesh, in_specs=(spec,) * 5, out_specs=(spec,) * 4, check_vma=False
    )
```

```python
import math

import jax
import jax.numpy as jnp
from jax import lax
from jax.experimental import pallas as pl
from jax.experimental.pallas import tpu as pltpu
from jax.sharding import PartitionSpec as P

D = 8192
QH = 32
KVH = 4
HD = 128
GROUP = QH // KVH
WIDE = GROUP * HD
TILE = 256
PART = 4 * HD
NEGATIVE = -1e30
BF16 = jnp.bfloat16
F32 = jnp.float32
VMEM_BYTES = 24 * 1024 * 1024
ALL_VMEM_BYTES = 62 * 1024 * 1024

NT = (((1,), (1,)), ((), ()))


def pack_kernel(rows, groups, halves, *refs):
    q_hbm, do_hbm, k_hbm, v_hbm, x_hbm, kv_out = refs[:6]
    piece_out = refs[6 : 5 + KVH]
    give_out, kv_s, piece_s, give_s, sems, out_sems = refs[5 + KVH :]
    head = lax.axis_index("seq") % KVH
    core = lax.axis_index("dp") % 2
    width = give_s.shape[1] // halves

    def of(index, block):
        return pl.ds(pl.multiple_of(index * block, block), block)

    loads = []

    def load(copies):
        made = []
        for source, target in copies:
            made.append(pltpu.make_async_copy(source, target, sems.at[len(loads)]))
            made[-1].start()
            loads.append(made[-1])
        return made

    small = load(
        (
            array.at[:, k * HD : (k + 1) * HD],
            kv_s.at[group * KVH + k, :, kind * HD : (kind + 1) * HD],
        )
        for k in range(KVH)
        for group in range(groups)
        for kind, array in enumerate((k_hbm, v_hbm))
    )
    large = [
        load(
            (
                array.at[:, of(head ^ k, WIDE)],
                piece_s.at[k - 1, :, kind * WIDE : (kind + 1) * WIDE],
            )
            for kind, array in enumerate((q_hbm, do_hbm))
        )
        for k in range(1, KVH)
    ]
    give = load(
        (
            x_hbm.at[:, of(2 * half + 1 - core, width)],
            give_s.at[:, half * width : (half + 1) * width],
        )
        for half in range(halves)
    )
    outs = []

    def pass_on(copies, source, target):
        for copy in copies:
            copy.wait()
        outs.append(pltpu.make_async_copy(source, target, out_sems.at[len(outs)]))
        outs[-1].start()

    pass_on(small, kv_s, kv_out)
    for k in range(1, KVH):
        pass_on(large[k - 1], piece_s.at[k - 1], piece_out[k - 1])
    pass_on(give, give_s, give_out)
    for copy in outs:
        copy.wait()


def packed(rows, groups, halves, queries, out_grad, key_states, value_states, layer_input):
    any_spec = pl.BlockSpec(memory_space=pltpu.HBM)
    cycle = KVH * groups
    outs = pl.pallas_call(
        lambda *refs: pack_kernel(rows, groups, halves, *refs),
        out_shape=[jax.ShapeDtypeStruct((cycle, rows, 2 * HD), BF16)]
        + [jax.ShapeDtypeStruct((rows, 2 * WIDE), BF16)] * (KVH - 1)
        + [jax.ShapeDtypeStruct((rows, D // 2), BF16)],
        in_specs=[any_spec] * 5,
        out_specs=[any_spec] * (KVH + 1),
        scratch_shapes=[
            pltpu.VMEM((cycle, rows, 2 * HD), BF16),
            pltpu.VMEM((KVH - 1, rows, 2 * WIDE), BF16),
            pltpu.VMEM((rows, D // 2), BF16),
            pltpu.SemaphoreType.DMA((2 * cycle + 2 * KVH + halves,)),
            pltpu.SemaphoreType.DMA((KVH + 1,)),
        ],
        compiler_params=pltpu.CompilerParams(vmem_limit_bytes=ALL_VMEM_BYTES),
        cost_estimate=pl.CostEstimate(flops=0, bytes_accessed=8 * 10**6, transcendentals=0),
        name="first_sends",
    )(queries, out_grad, key_states, value_states, layer_input)
    return outs[0], outs[1:KVH], outs[KVH]


def column_blocks(halves, groups, k):
    place = lax.axis_index("seq")
    group = place // KVH
    head = place % KVH
    half = lax.axis_index("dp") // 2
    core = lax.axis_index("dp") % 2
    blocks = []
    for apart in range(halves):
        for step in range(groups):
            mine = (((half ^ apart) * 2 + core) * groups + (group ^ step)) * KVH + (head ^ k)
            given = ((half ^ apart) * groups + (group ^ step)) * KVH + (head ^ k)
            blocks.append((mine, given))
    return blocks


def column_kernel(rows, halves, groups, slab, *refs):
    x_hbm, given_hbm = refs[:2]
    outs = refs[2 : 2 + KVH]
    x_s, sems, out_sems = refs[2 + KVH :]
    loads = []
    for k in range(KVH):
        for b, places in enumerate(column_blocks(halves, groups, k)):
            for which, source in enumerate((x_hbm, given_hbm)):
                loads.append(
                    pltpu.make_async_copy(
                        source.at[:, pl.ds(pl.multiple_of(places[which] * slab, slab), slab)],
                        x_s.at[k, which * rows : (which + 1) * rows, b * slab : (b + 1) * slab],
                        sems.at[len(loads)],
                    )
                )
    for load in loads:
        load.start()
    stores = []
    each = len(loads) // KVH
    for k in range(KVH):
        for load in loads[k * each : (k + 1) * each]:
            load.wait()
        stores.append(pltpu.make_async_copy(x_s.at[k], outs[k], out_sems.at[k]))
        stores[-1].start()
    for store in stores:
        store.wait()


def columns_for_group(rows, halves, groups, slab, layer_input, given):
    width = halves * groups * slab
    if slab % HD:
        return [
            jnp.concatenate(
                [
                    jnp.concatenate(
                        [
                            lax.dynamic_slice_in_dim(array, places[which] * slab, slab, 1)
                            for places in column_blocks(halves, groups, k)
                        ],
                        axis=1,
                    )
                    for which, array in enumerate((layer_input, given))
                ],
                axis=0,
            )
            for k in range(KVH)
        ]
    any_spec = pl.BlockSpec(memory_space=pltpu.HBM)
    return pl.pallas_call(
        lambda *refs: column_kernel(rows, halves, groups, slab, *refs),
        out_shape=[jax.ShapeDtypeStruct((2 * rows, width), BF16)] * KVH,
        in_specs=[any_spec] * 2,
        out_specs=[any_spec] * KVH,
        scratch_shapes=[
            pltpu.VMEM((KVH, 2 * rows, width), BF16),
            pltpu.SemaphoreType.DMA((2 * KVH * halves * groups,)),
            pltpu.SemaphoreType.DMA((KVH,)),
        ],
        compiler_params=pltpu.CompilerParams(vmem_limit_bytes=ALL_VMEM_BYTES),
        cost_estimate=pl.CostEstimate(flops=0, bytes_accessed=8 * 10**6, transcendentals=0),
        name="input_columns",
    )(layer_input, given)


def attention_kernel(rows, groups, *refs):
    span = KVH * rows
    q_hbm, do_hbm, kv_hbm = refs[:3]
    pieces = refs[3 : 3 + KVH - 1]
    at = 3 + KVH - 1
    dq_out = refs[at : at + KVH]
    at += KVH
    own_out = refs[at]
    at += 1
    down_out = refs[at : at + groups - 1]
    at += groups - 1
    q_s, do_s, dq_s, k_s, v_s, kt_s, dk_s, dv_s, down_s, sems, q_sems, dq_sems = refs[at:]

    place = lax.axis_index("seq")
    group = place // KVH
    head = place % KVH

    def row_at(k, base=0):
        return pl.ds(pl.multiple_of(base + (head ^ k) * rows, rows), rows)

    def column_at(block):
        return pl.ds(pl.multiple_of(head * block, block), block)

    def loads(chunk):
        first = chunk * PART
        made = []
        for k in range(KVH):
            for kind, target in enumerate((q_s, do_s)):
                if k:
                    source = pieces[k - 1].at[:, pl.ds(pl.multiple_of(kind * WIDE + first, PART), PART)]
                else:
                    source = (q_hbm, do_hbm)[kind].at[
                        :, pl.ds(pl.multiple_of(head * WIDE + first, PART), PART)
                    ]
                made.append(
                    pltpu.make_async_copy(
                        source,
                        target.at[row_at(k), pl.ds(pl.multiple_of(first, PART), PART)],
                        q_sems.at[chunk, 2 * k + kind],
                    )
                )
        return made

    def stores(chunk):
        columns = pl.ds(pl.multiple_of(chunk * PART, PART), PART)
        return [
            pltpu.make_async_copy(
                dq_s.at[row_at(k), columns], dq_out[k].at[:, columns], dq_sems.at[chunk, k]
            )
            for k in range(KVH)
        ]

    copies = []
    for kind, target in enumerate((k_s, v_s)):
        copies += [
            pltpu.make_async_copy(
                kv_hbm.at[source, :, kind * HD : (kind + 1) * HD],
                target.at[source * rows : (source + 1) * rows],
                sems.at[2 * source + kind],
            )
            for source in range(KVH * groups)
        ]
    for copy in copies + loads(0):
        copy.start()
    for chunk in range(1, WIDE // PART):
        for copy in loads(chunk):
            copy.start()
    for copy in copies:
        copy.wait()

    dk_s[...] = jnp.zeros_like(dk_s)
    dv_s[...] = jnp.zeros_like(dv_s)
    scale = 1.0 / math.sqrt(HD)
    fold = scale * math.log2(math.e)

    for which in range(groups):

        @pl.when(group == which)
        def _(which=which):
            for block in range((which + 1) * span // TILE):
                keys = slice(block * TILE, (block + 1) * TILE)
                kt_s[:, keys] = k_s[keys, :].T

            def one_head(h, carry):
                columns = pl.ds(pl.multiple_of(h * HD, HD), HD)
                for part in range(span // TILE):
                    q = q_s[part * TILE : (part + 1) * TILE, columns]
                    do = do_s[part * TILE : (part + 1) * TILE, columns]
                    length = which * span + (part + 1) * TILE
                    blocks = length // TILE
                    scores = []
                    grads = []
                    for b in range(blocks):
                        keys = slice(b * TILE, (b + 1) * TILE)
                        one = lax.dot_general(k_s[keys, :], q, NT, preferred_element_type=F32)
                        if b == blocks - 1:
                            key_place = lax.broadcasted_iota(jnp.int32, (TILE, TILE), 0)
                            query_place = lax.broadcasted_iota(jnp.int32, (TILE, TILE), 1)
                            one = jnp.where(key_place <= query_place, one, NEGATIVE)
                        scores.append(one)
                        grads.append(
                            lax.dot_general(v_s[keys, :], do, NT, preferred_element_type=F32)
                        )
                    top = scores[0].max(axis=0, keepdims=True)
                    for one in scores[1:]:
                        top = jnp.maximum(top, one.max(axis=0, keepdims=True))
                    expon = [jnp.exp2((one - top) * fold) for one in scores]
                    denom = sum(e.sum(axis=0, keepdims=True) for e in expon)
                    weighted = sum(
                        (e * gp).sum(axis=0, keepdims=True) for e, gp in zip(expon, grads)
                    )
                    inverse = 1.0 / denom
                    delta = weighted * inverse
                    probs = jnp.concatenate([(e * inverse).astype(BF16) for e in expon], axis=0)
                    grad_scores = jnp.concatenate(
                        [
                            (e * (inverse * scale) * (gp - delta)).astype(BF16)
                            for e, gp in zip(expon, grads)
                        ],
                        axis=0,
                    )
                    dv_s[:length, :] += jnp.dot(probs, do, preferred_element_type=F32)
                    dk_s[:length, :] += jnp.dot(grad_scores, q, preferred_element_type=F32)
                    dqt = jnp.dot(kt_s[:, :length], grad_scores, preferred_element_type=F32)
                    dq_s[part * TILE : (part + 1) * TILE, columns] = dqt.T.astype(BF16)
                return carry

            def one_chunk(chunk, carry):
                for copy in loads(chunk):
                    copy.wait()
                for h in range(PART // HD):
                    one_head(chunk * (PART // HD) + h, 0)
                for copy in stores(chunk):
                    copy.start()
                return carry

            lax.fori_loop(0, WIDE // PART, one_chunk, 0)
            base = which * span
            own_out[:, :HD] = dk_s[base : base + span, :]
            own_out[:, HD:] = dv_s[base : base + span, :]
            for step in range(1, which + 1):
                source = (which - step) * span
                down_s[step - 1, :, :HD] = dk_s[source : source + span, :].astype(BF16)
                down_s[step - 1, :, HD:] = dv_s[source : source + span, :].astype(BF16)
            for step in range(which + 1, groups):
                down_s[step - 1] = jnp.zeros((span, 2 * HD), BF16)

    outs = [
        pltpu.make_async_copy(down_s.at[step], down_out[step], sems.at[step])
        for step in range(groups - 1)
    ]
    for copy in outs:
        copy.start()
    for chunk in range(WIDE // PART):
        outs += stores(chunk)
    for copy in outs:
        copy.wait()


def attention(rows, groups, queries, out_grad, keys_values, pieces):
    span = KVH * rows
    length = groups * span
    any_spec = pl.BlockSpec(memory_space=pltpu.HBM)
    n_in = 3 + len(pieces)
    out_shape = (
        [jax.ShapeDtypeStruct((rows, WIDE), BF16)] * KVH
        + [jax.ShapeDtypeStruct((span, 2 * HD), F32)]
        + [jax.ShapeDtypeStruct((span, 2 * HD), BF16)] * (groups - 1)
    )
    out_specs = (
        [any_spec] * KVH
        + [pl.BlockSpec(memory_space=pltpu.VMEM)]
        + [any_spec] * (groups - 1)
    )
    outs = pl.pallas_call(
        lambda *refs: attention_kernel(rows, groups, *refs),
        out_shape=out_shape,
        in_specs=[any_spec] * n_in,
        out_specs=out_specs,
        scratch_shapes=[
            pltpu.VMEM((span, WIDE), BF16),
            pltpu.VMEM((span, WIDE), BF16),
            pltpu.VMEM((span, WIDE), BF16),
            pltpu.VMEM((length, HD), BF16),
            pltpu.VMEM((length, HD), BF16),
            pltpu.VMEM((HD, length), BF16),
            pltpu.VMEM((length, HD), F32),
            pltpu.VMEM((length, HD), F32),
            pltpu.VMEM((max(groups - 1, 1), span, 2 * HD), BF16),
            pltpu.SemaphoreType.DMA((2 * KVH * groups,)),
            pltpu.SemaphoreType.DMA((WIDE // PART, 2 * KVH)),
            pltpu.SemaphoreType.DMA((WIDE // PART, KVH)),
        ],
        compiler_params=pltpu.CompilerParams(vmem_limit_bytes=ALL_VMEM_BYTES),
        cost_estimate=pl.CostEstimate(flops=10**10, bytes_accessed=5 * 10**7, transcendentals=0),
        name="attention",
    )(queries, out_grad, keys_values, *pieces)
    return outs[:KVH], outs[KVH], outs[KVH + 1 :]


def products(x, g_s, block, slab):
    left = jnp.concatenate([x[k][:, block : block + slab].T for k in range(KVH)], axis=1)
    return jnp.dot(left, g_s[...], preferred_element_type=F32)


def away_kernel(rows, halves, groups, slab, *refs):
    own = refs[:KVH]
    other = refs[KVH : 2 * KVH]
    x = refs[2 * KVH : 3 * KVH]
    at = 3 * KVH
    away = (refs[at : at + groups - 1], refs[at + groups - 1 : at + 2 * groups - 2])
    mine_out = refs[at + 2 * groups - 2 : at + 2 * groups]
    g_s = refs[-1]
    width = KVH * HD
    head = lax.axis_index("seq") % KVH
    mine = pl.ds(pl.multiple_of(head * rows, rows), rows)
    for k in range(KVH):
        for kind in range(2):
            part = slice(kind * HD, (kind + 1) * HD)
            columns = pl.ds(pl.multiple_of((head ^ k) * HD, HD), HD)
            wide = pl.ds(pl.multiple_of(kind * width + (head ^ k) * HD, HD), HD)
            mine_out[kind][:, columns] = own[k][mine, part]
            for far in range(KVH):
                lines = pl.ds(pl.multiple_of((head ^ far) * rows, rows), rows)
                first = 2 * far * rows
                g_s[first : first + rows, wide] = own[k][lines, part]
                g_s[first + rows : first + 2 * rows, wide] = other[k][lines, part]
    for apart in range(1, halves):
        for step in range(1, groups):
            product = products(x, g_s, (apart * groups + step) * slab, slab)
            lines = slice((apart - 1) * slab, apart * slab)
            for kind in range(2):
                away[kind][step - 1][lines, :] = product[
                    :, kind * width : (kind + 1) * width
                ].astype(BF16)


def away_terms(rows, halves, groups, slab, own, other, inputs):
    span = KVH * rows
    channels = KVH * HD
    vmem = pl.BlockSpec(memory_space=pltpu.VMEM)
    others = max(halves - 1, 1) * slab
    outs = pl.pallas_call(
        lambda *refs: away_kernel(rows, halves, groups, slab, *refs),
        out_shape=[jax.ShapeDtypeStruct((others, channels), BF16)] * (2 * (groups - 1))
        + [jax.ShapeDtypeStruct((rows, channels), BF16)] * 2
        + [jax.ShapeDtypeStruct((2 * span, 2 * channels), BF16)],
        in_specs=[vmem] * (3 * KVH),
        out_specs=[vmem] * (2 * groups + 1),
        compiler_params=pltpu.CompilerParams(vmem_limit_bytes=VMEM_BYTES),
        cost_estimate=pl.CostEstimate(flops=10**9, bytes_accessed=6 * 10**6, transcendentals=0),
        name="weight_terms_away",
    )(*own, *other, *inputs)
    at = groups - 1
    return (outs[:at], outs[at : 2 * at]), outs[2 * at : 2 * at + 2], outs[-1]


def near_kernel(halves, groups, slab, *refs):
    x = refs[:KVH]
    g_s, keep, same = refs[KVH:]
    for step in range(groups - 1, -1, -1):
        keep[step * slab : (step + 1) * slab, :] = products(x, g_s, step * slab, slab)
    for apart in range(1, halves):
        product = products(x, g_s, apart * groups * slab, slab)
        same[(apart - 1) * slab : apart * slab, :] = product.astype(BF16)


def near_terms(halves, groups, slab, inputs, joined_grads):
    channels = joined_grads.shape[1]
    vmem = pl.BlockSpec(memory_space=pltpu.VMEM)
    return pl.pallas_call(
        lambda *refs: near_kernel(halves, groups, slab, *refs),
        out_shape=[
            jax.ShapeDtypeStruct((groups * slab, channels), F32),
            jax.ShapeDtypeStruct((max(halves - 1, 1) * slab, channels), BF16),
        ],
        in_specs=[vmem] * (KVH + 1),
        out_specs=[vmem] * 2,
        compiler_params=pltpu.CompilerParams(vmem_limit_bytes=VMEM_BYTES),
        cost_estimate=pl.CostEstimate(flops=2 * 10**9, bytes_accessed=6 * 10**6, transcendentals=0),
        name="weight_terms_near",
    )(*inputs, joined_grads)


def place_kernel(*refs):
    out = refs[KVH]
    head = lax.axis_index("seq") % KVH
    for k in range(KVH):
        out[:, pl.ds(pl.multiple_of((head ^ k) * WIDE, WIDE), WIDE)] = refs[k][...]


def placed(rows, pieces):
    vmem = pl.BlockSpec(memory_space=pltpu.VMEM)
    return pl.pallas_call(
        place_kernel,
        out_shape=jax.ShapeDtypeStruct((rows, QH * HD), BF16),
        in_specs=[vmem] * KVH,
        out_specs=vmem,
        compiler_params=pltpu.CompilerParams(vmem_limit_bytes=VMEM_BYTES),
        cost_estimate=pl.CostEstimate(flops=0, bytes_accessed=5 * 10**6, transcendentals=0),
        name="query_grad_placed",
    )(*pieces)


def add_kernel(kind, step, keep, *refs):
    out = refs[-1]
    slab, width = out.shape
    total = keep[step * slab : (step + 1) * slab, kind * width : (kind + 1) * width]
    for ref in refs[:-1]:
        total = total + ref[...].astype(F32)
    out[...] = total.astype(BF16)


def added(keep, parts, kind, step):
    vmem = pl.BlockSpec(memory_space=pltpu.VMEM)
    return pl.pallas_call(
        lambda *refs: add_kernel(kind, step, *refs),
        out_shape=jax.ShapeDtypeStruct(parts[0].shape, BF16),
        in_specs=[vmem] * (1 + len(parts)),
        out_specs=vmem,
        compiler_params=pltpu.CompilerParams(vmem_limit_bytes=VMEM_BYTES),
        cost_estimate=pl.CostEstimate(flops=0, bytes_accessed=10**6, transcendentals=0),
        name="sequences_added",
    )(keep, *parts)


def join_kernel(wide, *refs):
    keep = refs[0]
    both = refs[1 : 1 + wide]
    out = refs[-1]
    rest = refs[1 + wide : -1]
    count = len(rest) // 2
    slab, width = out.shape[0], out.shape[1] // 2
    for kind in range(2):
        at = slice(kind * width, (kind + 1) * width)
        total = keep[:slab, at]
        for ref in both:
            total = total + ref[:, at].astype(F32)
        for ref in rest[kind * count : (kind + 1) * count]:
            total = total + ref[...].astype(F32)
        out[:, at] = total


def joined(slab, keep, both, rest):
    vmem = pl.BlockSpec(memory_space=pltpu.VMEM)
    return pl.pallas_call(
        lambda *refs: join_kernel(len(both), *refs),
        out_shape=jax.ShapeDtypeStruct((slab, keep.shape[1]), F32),
        in_specs=[vmem] * (1 + len(both) + len(rest)),
        out_specs=vmem,
        compiler_params=pltpu.CompilerParams(vmem_limit_bytes=VMEM_BYTES),
        cost_estimate=pl.CostEstimate(flops=0, bytes_accessed=3 * 10**6, transcendentals=0),
        name="weight_grad_joined",
    )(keep, *both, *rest)


def local(layer_input, queries, key_states, value_states, out_grad):
    rows = layer_input.shape[0]
    cycle = lax.axis_size("seq")
    replicas = lax.axis_size("dp")
    groups = cycle // KVH
    halves = replicas // 2
    slab = D // (replicas * cycle)
    after = lax.optimization_barrier
    within = [[i + k for k in range(KVH)] for i in range(0, cycle, KVH)]

    def swap(array, k):
        return lax.ppermute(array, "seq", [(i, i ^ k) for i in range(cycle)])

    def across_cores(array):
        return lax.ppermute(array, "dp", [(i, i ^ 1) for i in range(replicas)])

    def exchange(array, parts=None):
        return lax.all_to_all(
            array, "seq", split_axis=0, concat_axis=0, tiled=True, axis_index_groups=parts
        )

    keys_values, sends, give = packed(
        rows, groups, halves, queries, out_grad, key_states, value_states, layer_input
    )
    keys_values = exchange(keys_values)
    pieces = [None] * KVH
    for k in range(KVH - 1, 0, -1):
        pieces[k] = swap(sends[k - 1], k)
    pieces = pieces[1:]

    columns = columns_for_group(rows, halves, groups, slab, layer_input, across_cores(give))
    columns, pieces = after((columns, pieces))
    inputs = [columns[0]] + [swap(columns[k], k) for k in range(1, KVH)]

    grads, own, down = attention(rows, groups, queries, out_grad, keys_values, pieces)
    inputs[1:], down = after((inputs[1:], down))

    received = [
        lax.ppermute(
            down[step - 1], "seq", [(i + step * KVH, i) for i in range(cycle - step * KVH)]
        )
        for step in range(1, groups)
    ]
    returned = [grads[0], swap(grads[1], 1), swap(grads[2], 2), None]
    received, returned[:3] = after((received, returned[:3]))
    total = own
    for part in received:
        total = total + part.astype(F32)
    total = total.astype(BF16)
    gathered = [total] + [swap(total, k) for k in range(1, KVH)]
    others = [across_cores(piece) for piece in gathered]
    away, narrow, joined_grads = away_terms(
        rows, halves, groups, slab, gathered, others, inputs
    )
    keep, same = near_terms(halves, groups, slab, inputs, joined_grads)

    def over_sequences(array):
        return [
            lax.ppermute(
                array[(apart - 1) * slab : apart * slab],
                "dp",
                [(i, i ^ (2 * apart)) for i in range(replicas)],
            )
            for apart in range(1, halves)
        ]

    parts = [[over_sequences(array) for array in away[kind]] for kind in range(2)]
    returned[3] = swap(grads[3], 3)

    totals = [None, None]
    rest = [None, None]
    for kind in (1, 0):
        if not kind:
            parts[0], _ = after((parts[0], returned[3]))
        totals[kind] = [
            added(keep, parts[kind][step - 1], kind, step) for step in range(1, groups)
        ]
        rest[kind] = [swap(total, (step + 1) * KVH) for step, total in enumerate(totals[kind])]
    weight_grad = joined(slab, keep, over_sequences(same), rest[0] + rest[1])
    query_grad = placed(rows, returned)
    return (query_grad, narrow[0], narrow[1], weight_grad)


def solution(mesh):
    spec = P(("dp", "seq"), None)
    return jax.shard_map(
        local, mesh=mesh, in_specs=(spec,) * 5, out_specs=(spec,) * 4, check_vma=False
    )
```

```python
import math

import jax
import jax.numpy as jnp
from jax import lax
from jax.experimental import pallas as pl
from jax.experimental.pallas import tpu as pltpu
from jax.sharding import PartitionSpec as P

D = 8192
QH = 32
KVH = 4
HD = 128
GROUP = QH // KVH
WIDE = GROUP * HD
TILE = 256
PART = 4 * HD
NEGATIVE = -1e30
BF16 = jnp.bfloat16
F32 = jnp.float32
VMEM_BYTES = 24 * 1024 * 1024
ALL_VMEM_BYTES = 62 * 1024 * 1024
ATTENTION_VMEM_BYTES = 40 * 1024 * 1024

NT = (((1,), (1,)), ((), ()))


def pack_kernel(rows, groups, halves, *refs):
    q_hbm, do_hbm, k_hbm, v_hbm, x_hbm, kv_out = refs[:6]
    piece_out = refs[6 : 5 + KVH]
    give_out, kv_s, piece_s, give_s, sems, out_sems = refs[5 + KVH :]
    head = lax.axis_index("seq") % KVH
    core = lax.axis_index("dp") % 2
    width = give_s.shape[1] // halves

    def of(index, block):
        return pl.ds(pl.multiple_of(index * block, block), block)

    loads = []

    def load(copies):
        made = []
        for source, target in copies:
            made.append(pltpu.make_async_copy(source, target, sems.at[len(loads)]))
            made[-1].start()
            loads.append(made[-1])
        return made

    small = load(
        (
            array.at[:, k * HD : (k + 1) * HD],
            kv_s.at[group * KVH + k, :, kind * HD : (kind + 1) * HD],
        )
        for k in range(KVH)
        for group in range(groups)
        for kind, array in enumerate((k_hbm, v_hbm))
    )
    large = [
        load(
            (
                array.at[:, of(head ^ k, WIDE)],
                piece_s.at[k - 1, :, kind * WIDE : (kind + 1) * WIDE],
            )
            for kind, array in enumerate((q_hbm, do_hbm))
        )
        for k in range(1, KVH)
    ]
    give = load(
        (
            x_hbm.at[:, of(2 * half + 1 - core, width)],
            give_s.at[:, half * width : (half + 1) * width],
        )
        for half in range(halves)
    )
    outs = []

    def pass_on(copies, source, target):
        for copy in copies:
            copy.wait()
        outs.append(pltpu.make_async_copy(source, target, out_sems.at[len(outs)]))
        outs[-1].start()

    pass_on(small, kv_s, kv_out)
    for k in range(1, KVH):
        pass_on(large[k - 1], piece_s.at[k - 1], piece_out[k - 1])
    pass_on(give, give_s, give_out)
    for copy in outs:
        copy.wait()


def packed(rows, groups, halves, queries, out_grad, key_states, value_states, layer_input):
    any_spec = pl.BlockSpec(memory_space=pltpu.HBM)
    cycle = KVH * groups
    outs = pl.pallas_call(
        lambda *refs: pack_kernel(rows, groups, halves, *refs),
        out_shape=[jax.ShapeDtypeStruct((cycle, rows, 2 * HD), BF16)]
        + [jax.ShapeDtypeStruct((rows, 2 * WIDE), BF16)] * (KVH - 1)
        + [jax.ShapeDtypeStruct((rows, D // 2), BF16)],
        in_specs=[any_spec] * 5,
        out_specs=[any_spec] * (KVH + 1),
        scratch_shapes=[
            pltpu.VMEM((cycle, rows, 2 * HD), BF16),
            pltpu.VMEM((KVH - 1, rows, 2 * WIDE), BF16),
            pltpu.VMEM((rows, D // 2), BF16),
            pltpu.SemaphoreType.DMA((2 * cycle + 2 * KVH + halves,)),
            pltpu.SemaphoreType.DMA((KVH + 1,)),
        ],
        compiler_params=pltpu.CompilerParams(vmem_limit_bytes=ALL_VMEM_BYTES),
        cost_estimate=pl.CostEstimate(flops=0, bytes_accessed=8 * 10**6, transcendentals=0),
        name="first_sends",
    )(queries, out_grad, key_states, value_states, layer_input)
    return outs[0], outs[1:KVH], outs[KVH]


def column_blocks(halves, groups, k):
    place = lax.axis_index("seq")
    group = place // KVH
    head = place % KVH
    half = lax.axis_index("dp") // 2
    core = lax.axis_index("dp") % 2
    blocks = []
    for apart in range(halves):
        for step in range(groups):
            mine = (((half ^ apart) * 2 + core) * groups + (group ^ step)) * KVH + (head ^ k)
            given = ((half ^ apart) * groups + (group ^ step)) * KVH + (head ^ k)
            blocks.append((mine, given))
    return blocks


def column_kernel(rows, halves, groups, slab, *refs):
    x_hbm, given_hbm = refs[:2]
    outs = refs[2 : 2 + KVH]
    x_s, sems, out_sems = refs[2 + KVH :]
    loads = []
    for k in range(KVH):
        for b, places in enumerate(column_blocks(halves, groups, k)):
            for which, source in enumerate((x_hbm, given_hbm)):
                loads.append(
                    pltpu.make_async_copy(
                        source.at[:, pl.ds(pl.multiple_of(places[which] * slab, slab), slab)],
                        x_s.at[k, which * rows : (which + 1) * rows, b * slab : (b + 1) * slab],
                        sems.at[len(loads)],
                    )
                )
    for load in loads:
        load.start()
    stores = []
    each = len(loads) // KVH
    for k in range(KVH):
        for load in loads[k * each : (k + 1) * each]:
            load.wait()
        stores.append(pltpu.make_async_copy(x_s.at[k], outs[k], out_sems.at[k]))
        stores[-1].start()
    for store in stores:
        store.wait()


def columns_for_group(rows, halves, groups, slab, layer_input, given):
    width = halves * groups * slab
    if slab % HD:
        return [
            jnp.concatenate(
                [
                    jnp.concatenate(
                        [
                            lax.dynamic_slice_in_dim(array, places[which] * slab, slab, 1)
                            for places in column_blocks(halves, groups, k)
                        ],
                        axis=1,
                    )
                    for which, array in enumerate((layer_input, given))
                ],
                axis=0,
            )
            for k in range(KVH)
        ]
    any_spec = pl.BlockSpec(memory_space=pltpu.HBM)
    return pl.pallas_call(
        lambda *refs: column_kernel(rows, halves, groups, slab, *refs),
        out_shape=[jax.ShapeDtypeStruct((2 * rows, width), BF16)] * KVH,
        in_specs=[any_spec] * 2,
        out_specs=[any_spec] * KVH,
        scratch_shapes=[
            pltpu.VMEM((KVH, 2 * rows, width), BF16),
            pltpu.SemaphoreType.DMA((2 * KVH * halves * groups,)),
            pltpu.SemaphoreType.DMA((KVH,)),
        ],
        compiler_params=pltpu.CompilerParams(vmem_limit_bytes=ALL_VMEM_BYTES),
        cost_estimate=pl.CostEstimate(flops=0, bytes_accessed=8 * 10**6, transcendentals=0),
        name="input_columns",
    )(layer_input, given)


def attention_kernel(rows, groups, *refs):
    span = KVH * rows
    q_hbm, do_hbm, kv_hbm = refs[:3]
    pieces = refs[3 : 3 + KVH - 1]
    at = 3 + KVH - 1
    dq_out = refs[at : at + KVH]
    at += KVH
    own_out = refs[at]
    at += 1
    down_out = refs[at : at + groups - 1]
    at += groups - 1
    q_s, do_s, dq_s, k_s, v_s, kt_s, dk_s, dv_s, down_s, sems, q_sems, dq_sems = refs[at:]

    place = lax.axis_index("seq")
    group = place // KVH
    head = place % KVH

    def row_at(k, base=0):
        return pl.ds(pl.multiple_of(base + (head ^ k) * rows, rows), rows)

    def column_at(block):
        return pl.ds(pl.multiple_of(head * block, block), block)

    def loads(chunk):
        first = chunk * PART
        made = []
        for k in range(KVH):
            for kind, target in enumerate((q_s, do_s)):
                if k:
                    source = pieces[k - 1].at[:, pl.ds(pl.multiple_of(kind * WIDE + first, PART), PART)]
                else:
                    source = (q_hbm, do_hbm)[kind].at[
                        :, pl.ds(pl.multiple_of(head * WIDE + first, PART), PART)
                    ]
                made.append(
                    pltpu.make_async_copy(
                        source,
                        target.at[row_at(k), pl.ds(pl.multiple_of(first, PART), PART)],
                        q_sems.at[chunk, 2 * k + kind],
                    )
                )
        return made

    def stores(chunk):
        columns = pl.ds(pl.multiple_of(chunk * PART, PART), PART)
        return [
            pltpu.make_async_copy(
                dq_s.at[row_at(k), columns], dq_out[k].at[:, columns], dq_sems.at[chunk, k]
            )
            for k in range(KVH)
        ]

    copies = []
    for kind, target in enumerate((k_s, v_s)):
        copies += [
            pltpu.make_async_copy(
                kv_hbm.at[source, :, kind * HD : (kind + 1) * HD],
                target.at[source * rows : (source + 1) * rows],
                sems.at[2 * source + kind],
            )
            for source in range(KVH * groups)
        ]
    for copy in copies + loads(0):
        copy.start()
    for chunk in range(1, WIDE // PART):
        for copy in loads(chunk):
            copy.start()
    for copy in copies:
        copy.wait()

    dk_s[...] = jnp.zeros_like(dk_s)
    dv_s[...] = jnp.zeros_like(dv_s)
    scale = 1.0 / math.sqrt(HD)
    fold = scale * math.log2(math.e)

    for which in range(groups):

        @pl.when(group == which)
        def _(which=which):
            for block in range((which + 1) * span // TILE):
                keys = slice(block * TILE, (block + 1) * TILE)
                kt_s[:, keys] = k_s[keys, :].T

            def one_head(h, carry):
                columns = pl.ds(pl.multiple_of(h * HD, HD), HD)
                for part in range(span // TILE):
                    q = q_s[part * TILE : (part + 1) * TILE, columns]
                    do = do_s[part * TILE : (part + 1) * TILE, columns]
                    length = which * span + (part + 1) * TILE
                    blocks = length // TILE
                    scores = []
                    grads = []
                    for b in range(blocks):
                        keys = slice(b * TILE, (b + 1) * TILE)
                        one = lax.dot_general(k_s[keys, :], q, NT, preferred_element_type=F32)
                        if b == blocks - 1:
                            key_place = lax.broadcasted_iota(jnp.int32, (TILE, TILE), 0)
                            query_place = lax.broadcasted_iota(jnp.int32, (TILE, TILE), 1)
                            one = jnp.where(key_place <= query_place, one, NEGATIVE)
                        scores.append(one)
                        grads.append(
                            lax.dot_general(v_s[keys, :], do, NT, preferred_element_type=F32)
                        )
                    top = scores[0].max(axis=0, keepdims=True)
                    for one in scores[1:]:
                        top = jnp.maximum(top, one.max(axis=0, keepdims=True))
                    expon = [jnp.exp2((one - top) * fold) for one in scores]
                    denom = sum(e.sum(axis=0, keepdims=True) for e in expon)
                    weighted = sum(
                        (e * gp).sum(axis=0, keepdims=True) for e, gp in zip(expon, grads)
                    )
                    inverse = 1.0 / denom
                    delta = weighted * inverse
                    probs = jnp.concatenate([(e * inverse).astype(BF16) for e in expon], axis=0)
                    grad_scores = jnp.concatenate(
                        [
                            (e * (inverse * scale) * (gp - delta)).astype(BF16)
                            for e, gp in zip(expon, grads)
                        ],
                        axis=0,
                    )
                    dv_s[:length, :] += jnp.dot(probs, do, preferred_element_type=F32)
                    dk_s[:length, :] += jnp.dot(grad_scores, q, preferred_element_type=F32)
                    dqt = jnp.dot(kt_s[:, :length], grad_scores, preferred_element_type=F32)
                    dq_s[part * TILE : (part + 1) * TILE, columns] = dqt.T.astype(BF16)
                return carry

            def one_chunk(chunk, carry):
                for copy in loads(chunk):
                    copy.wait()
                for h in range(PART // HD):
                    one_head(chunk * (PART // HD) + h, 0)
                for copy in stores(chunk):
                    copy.start()
                return carry

            lax.fori_loop(0, WIDE // PART, one_chunk, 0)
            base = which * span
            own_out[:, :HD] = dk_s[base : base + span, :]
            own_out[:, HD:] = dv_s[base : base + span, :]
            for step in range(1, which + 1):
                source = (which - step) * span
                down_s[step - 1, :, :HD] = dk_s[source : source + span, :].astype(BF16)
                down_s[step - 1, :, HD:] = dv_s[source : source + span, :].astype(BF16)
            for step in range(which + 1, groups):
                down_s[step - 1] = jnp.zeros((span, 2 * HD), BF16)

    outs = [
        pltpu.make_async_copy(down_s.at[step], down_out[step], sems.at[step])
        for step in range(groups - 1)
    ]
    for copy in outs:
        copy.start()
    for chunk in range(WIDE // PART):
        outs += stores(chunk)
    for copy in outs:
        copy.wait()


def attention(rows, groups, queries, out_grad, keys_values, pieces):
    span = KVH * rows
    length = groups * span
    any_spec = pl.BlockSpec(memory_space=pltpu.HBM)
    n_in = 3 + len(pieces)
    out_shape = (
        [jax.ShapeDtypeStruct((rows, WIDE), BF16)] * KVH
        + [jax.ShapeDtypeStruct((span, 2 * HD), F32)]
        + [jax.ShapeDtypeStruct((span, 2 * HD), BF16)] * (groups - 1)
    )
    out_specs = (
        [any_spec] * KVH
        + [pl.BlockSpec(memory_space=pltpu.VMEM)]
        + [any_spec] * (groups - 1)
    )
    outs = pl.pallas_call(
        lambda *refs: attention_kernel(rows, groups, *refs),
        out_shape=out_shape,
        in_specs=[any_spec] * n_in,
        out_specs=out_specs,
        scratch_shapes=[
            pltpu.VMEM((span, WIDE), BF16),
            pltpu.VMEM((span, WIDE), BF16),
            pltpu.VMEM((span, WIDE), BF16),
            pltpu.VMEM((length, HD), BF16),
            pltpu.VMEM((length, HD), BF16),
            pltpu.VMEM((HD, length), BF16),
            pltpu.VMEM((length, HD), F32),
            pltpu.VMEM((length, HD), F32),
            pltpu.VMEM((max(groups - 1, 1), span, 2 * HD), BF16),
            pltpu.SemaphoreType.DMA((2 * KVH * groups,)),
            pltpu.SemaphoreType.DMA((WIDE // PART, 2 * KVH)),
            pltpu.SemaphoreType.DMA((WIDE // PART, KVH)),
        ],
        compiler_params=pltpu.CompilerParams(vmem_limit_bytes=ATTENTION_VMEM_BYTES),
        cost_estimate=pl.CostEstimate(flops=10**10, bytes_accessed=5 * 10**7, transcendentals=0),
        name="attention",
    )(queries, out_grad, keys_values, *pieces)
    return outs[:KVH], outs[KVH], outs[KVH + 1 :]


def products(x, g_s, block, slab):
    left = jnp.concatenate([x[k][:, block : block + slab].T for k in range(KVH)], axis=1)
    return jnp.dot(left, g_s[...], preferred_element_type=F32)


def away_kernel(rows, halves, groups, slab, *refs):
    own = refs[:KVH]
    other = refs[KVH : 2 * KVH]
    x = refs[2 * KVH : 3 * KVH]
    at = 3 * KVH
    away = (refs[at : at + groups - 1], refs[at + groups - 1 : at + 2 * groups - 2])
    mine_out = refs[at + 2 * groups - 2 : at + 2 * groups]
    g_s = refs[-1]
    width = KVH * HD
    head = lax.axis_index("seq") % KVH
    mine = pl.ds(pl.multiple_of(head * rows, rows), rows)
    for k in range(KVH):
        for kind in range(2):
            part = slice(kind * HD, (kind + 1) * HD)
            columns = pl.ds(pl.multiple_of((head ^ k) * HD, HD), HD)
            wide = pl.ds(pl.multiple_of(kind * width + (head ^ k) * HD, HD), HD)
            mine_out[kind][:, columns] = own[k][mine, part]
            for far in range(KVH):
                lines = pl.ds(pl.multiple_of((head ^ far) * rows, rows), rows)
                first = 2 * far * rows
                g_s[first : first + rows, wide] = own[k][lines, part]
                g_s[first + rows : first + 2 * rows, wide] = other[k][lines, part]
    for apart in range(1, halves):
        for step in range(1, groups):
            product = products(x, g_s, (apart * groups + step) * slab, slab)
            lines = slice((apart - 1) * slab, apart * slab)
            for kind in range(2):
                away[kind][step - 1][lines, :] = product[
                    :, kind * width : (kind + 1) * width
                ].astype(BF16)


def away_terms(rows, halves, groups, slab, own, other, inputs):
    span = KVH * rows
    channels = KVH * HD
    vmem = pl.BlockSpec(memory_space=pltpu.VMEM)
    others = max(halves - 1, 1) * slab
    outs = pl.pallas_call(
        lambda *refs: away_kernel(rows, halves, groups, slab, *refs),
        out_shape=[jax.ShapeDtypeStruct((others, channels), BF16)] * (2 * (groups - 1))
        + [jax.ShapeDtypeStruct((rows, channels), BF16)] * 2
        + [jax.ShapeDtypeStruct((2 * span, 2 * channels), BF16)],
        in_specs=[vmem] * (3 * KVH),
        out_specs=[vmem] * (2 * groups + 1),
        compiler_params=pltpu.CompilerParams(vmem_limit_bytes=VMEM_BYTES),
        cost_estimate=pl.CostEstimate(flops=10**9, bytes_accessed=6 * 10**6, transcendentals=0),
        name="weight_terms_away",
    )(*own, *other, *inputs)
    at = groups - 1
    return (outs[:at], outs[at : 2 * at]), outs[2 * at : 2 * at + 2], outs[-1]


def near_kernel(halves, groups, slab, *refs):
    x = refs[:KVH]
    g_s, keep, same = refs[KVH:]
    for step in range(groups - 1, -1, -1):
        keep[step * slab : (step + 1) * slab, :] = products(x, g_s, step * slab, slab)
    for apart in range(1, halves):
        product = products(x, g_s, apart * groups * slab, slab)
        same[(apart - 1) * slab : apart * slab, :] = product.astype(BF16)


def near_terms(halves, groups, slab, inputs, joined_grads):
    channels = joined_grads.shape[1]
    vmem = pl.BlockSpec(memory_space=pltpu.VMEM)
    return pl.pallas_call(
        lambda *refs: near_kernel(halves, groups, slab, *refs),
        out_shape=[
            jax.ShapeDtypeStruct((groups * slab, channels), F32),
            jax.ShapeDtypeStruct((max(halves - 1, 1) * slab, channels), BF16),
        ],
        in_specs=[vmem] * (KVH + 1),
        out_specs=[vmem] * 2,
        compiler_params=pltpu.CompilerParams(vmem_limit_bytes=VMEM_BYTES),
        cost_estimate=pl.CostEstimate(flops=2 * 10**9, bytes_accessed=6 * 10**6, transcendentals=0),
        name="weight_terms_near",
    )(*inputs, joined_grads)


def place_kernel(*refs):
    out = refs[KVH]
    head = lax.axis_index("seq") % KVH
    for k in range(KVH):
        out[:, pl.ds(pl.multiple_of((head ^ k) * WIDE, WIDE), WIDE)] = refs[k][...]


def placed(rows, pieces):
    vmem = pl.BlockSpec(memory_space=pltpu.VMEM)
    return pl.pallas_call(
        place_kernel,
        out_shape=jax.ShapeDtypeStruct((rows, QH * HD), BF16),
        in_specs=[vmem] * KVH,
        out_specs=vmem,
        compiler_params=pltpu.CompilerParams(vmem_limit_bytes=VMEM_BYTES),
        cost_estimate=pl.CostEstimate(flops=0, bytes_accessed=5 * 10**6, transcendentals=0),
        name="query_grad_placed",
    )(*pieces)


def add_kernel(kind, step, keep, *refs):
    out = refs[-1]
    slab, width = out.shape
    total = keep[step * slab : (step + 1) * slab, kind * width : (kind + 1) * width]
    for ref in refs[:-1]:
        total = total + ref[...].astype(F32)
    out[...] = total.astype(BF16)


def added(keep, parts, kind, step):
    vmem = pl.BlockSpec(memory_space=pltpu.VMEM)
    return pl.pallas_call(
        lambda *refs: add_kernel(kind, step, *refs),
        out_shape=jax.ShapeDtypeStruct(parts[0].shape, BF16),
        in_specs=[vmem] * (1 + len(parts)),
        out_specs=vmem,
        compiler_params=pltpu.CompilerParams(vmem_limit_bytes=VMEM_BYTES),
        cost_estimate=pl.CostEstimate(flops=0, bytes_accessed=10**6, transcendentals=0),
        name="sequences_added",
    )(keep, *parts)


def join_kernel(wide, *refs):
    keep = refs[0]
    both = refs[1 : 1 + wide]
    out = refs[-1]
    rest = refs[1 + wide : -1]
    count = len(rest) // 2
    slab, width = out.shape[0], out.shape[1] // 2
    for kind in range(2):
        at = slice(kind * width, (kind + 1) * width)
        total = keep[:slab, at]
        for ref in both:
            total = total + ref[:, at].astype(F32)
        for ref in rest[kind * count : (kind + 1) * count]:
            total = total + ref[...].astype(F32)
        out[:, at] = total


def joined(slab, keep, both, rest):
    vmem = pl.BlockSpec(memory_space=pltpu.VMEM)
    return pl.pallas_call(
        lambda *refs: join_kernel(len(both), *refs),
        out_shape=jax.ShapeDtypeStruct((slab, keep.shape[1]), F32),
        in_specs=[vmem] * (1 + len(both) + len(rest)),
        out_specs=vmem,
        compiler_params=pltpu.CompilerParams(vmem_limit_bytes=VMEM_BYTES),
        cost_estimate=pl.CostEstimate(flops=0, bytes_accessed=3 * 10**6, transcendentals=0),
        name="weight_grad_joined",
    )(keep, *both, *rest)


def local(layer_input, queries, key_states, value_states, out_grad):
    rows = layer_input.shape[0]
    cycle = lax.axis_size("seq")
    replicas = lax.axis_size("dp")
    groups = cycle // KVH
    halves = replicas // 2
    slab = D // (replicas * cycle)
    after = lax.optimization_barrier
    within = [[i + k for k in range(KVH)] for i in range(0, cycle, KVH)]

    def swap(array, k):
        return lax.ppermute(array, "seq", [(i, i ^ k) for i in range(cycle)])

    def across_cores(array):
        return lax.ppermute(array, "dp", [(i, i ^ 1) for i in range(replicas)])

    def exchange(array, parts=None):
        return lax.all_to_all(
            array, "seq", split_axis=0, concat_axis=0, tiled=True, axis_index_groups=parts
        )

    keys_values, sends, give = packed(
        rows, groups, halves, queries, out_grad, key_states, value_states, layer_input
    )
    keys_values = exchange(keys_values)
    pieces = [None] * KVH
    for k in range(KVH - 1, 0, -1):
        pieces[k] = swap(sends[k - 1], k)
    pieces = pieces[1:]

    columns = columns_for_group(rows, halves, groups, slab, layer_input, across_cores(give))
    columns, pieces = after((columns, pieces))
    inputs = [columns[0]] + [swap(columns[k], k) for k in range(1, KVH)]

    grads, own, down = attention(rows, groups, queries, out_grad, keys_values, pieces)
    inputs[1:], down = after((inputs[1:], down))

    received = [
        lax.ppermute(
            down[step - 1], "seq", [(i + step * KVH, i) for i in range(cycle - step * KVH)]
        )
        for step in range(1, groups)
    ]
    returned = [grads[0], swap(grads[1], 1), swap(grads[2], 2), None]
    received, returned[:3] = after((received, returned[:3]))
    total = own
    for part in received:
        total = total + part.astype(F32)
    total = total.astype(BF16)
    gathered = [total] + [swap(total, k) for k in range(1, KVH)]
    others = [across_cores(piece) for piece in gathered]
    away, narrow, joined_grads = away_terms(
        rows, halves, groups, slab, gathered, others, inputs
    )
    keep, same = near_terms(halves, groups, slab, inputs, joined_grads)

    def over_sequences(array):
        return [
            lax.ppermute(
                array[(apart - 1) * slab : apart * slab],
                "dp",
                [(i, i ^ (2 * apart)) for i in range(replicas)],
            )
            for apart in range(1, halves)
        ]

    parts = [[over_sequences(array) for array in away[kind]] for kind in range(2)]
    returned[3] = swap(grads[3], 3)

    totals = [None, None]
    rest = [None, None]
    for kind in (1, 0):
        if not kind:
            parts[0], _ = after((parts[0], returned[3]))
        totals[kind] = [
            added(keep, parts[kind][step - 1], kind, step) for step in range(1, groups)
        ]
        rest[kind] = [swap(total, (step + 1) * KVH) for step, total in enumerate(totals[kind])]
    weight_grad = joined(slab, keep, over_sequences(same), rest[0] + rest[1])
    query_grad = placed(rows, returned)
    return (query_grad, narrow[0], narrow[1], weight_grad)


def solution(mesh):
    spec = P(("dp", "seq"), None)
    return jax.shard_map(
        local, mesh=mesh, in_specs=(spec,) * 5, out_specs=(spec,) * 4, check_vma=False
    )
```
